32 devices in a mesh: layer: 4 (over y, x), row: 2 (over core), col: 4 (over z).
Axes of the slice: x: 2, y: 2, z: 4, core: 2. Of those that a mesh axis runs over, the one named last changes fastest.
Arguments:
- blocks: bfloat16 [13, 512, 128, 128], P(None, ('row', 'col'), 'layer'), may hold values from -0.29882812 to 0.29882812
- presence: int32 [13, 512], P(None, ('row', 'col')), may hold values from 0 to 1, as said below
Outputs:
- purified: bfloat16 [13, 512, 128, 128], P(None, ('row', 'col'), 'layer')
The draws below stay inside these ranges and needn't reach their ends.
Inputs may be any that keep to these rules, and one draw needn't show every extreme that they name: `presence`: the tile on offset 0 is present in every block row.
All inputs are finite; a program needn't handle non-finite values.
Results may differ from the reference program's by a relative error of at most 0.01.
Values may be sent and summed in bfloat16 or wider, within the bound.
A program may use at most 320 MiB of HBM per device.

```python
import jax
import jax.numpy as jnp

BS = 128
NBG = 512
BAND = 3
FAR = 160
DIAGS = 13


def draw_presence(key, part):
    key_band, key_level, key_far = jax.random.split(key, 3)
    band_rows = (jax.random.randint(key_band, (2 * BAND + 1, NBG), 0, 8) < 7).astype(jnp.int32)
    band_rows = band_rows.at[BAND].set(1)
    levels = jax.random.randint(key_level, (NBG // 8,), 1, 8)
    levels = jnp.repeat(levels, 8)
    far_rows = (jax.random.randint(key_far, (6, NBG), 0, 8) < levels[None, :]).astype(jnp.int32)
    return jnp.concatenate([band_rows, far_rows], axis=0).astype(jnp.int32)


def block_levels(key, shape, cuts, smallest, high):
    def one(position, shards_of):
        heights = jax.random.uniform(jax.random.fold_in(jax.random.fold_in(key, 6), position), (shards_of,), jnp.float32, smallest / len(cuts), high / len(cuts))
        return jnp.repeat(jnp.exp(heights), shape[position] // shards_of).reshape((-1,) + (1,) * (len(shape) - position - 1))

    factor_of = one(*cuts[0])
    for cut in cuts[1:]:
        factor_of = factor_of * one(*cut)
    return factor_of


def normal_values(key, shape, width, limit, cuts=(), held_as=jnp.bfloat16):
    result = width * jax.random.normal(key, shape, jnp.float32)
    if cuts:
        result = result * block_levels(key, shape, cuts, -0.22, 0.18)
    return jnp.clip(result, -limit, limit).astype(held_as)


def setup_inputs(seed: int = 0) -> dict:
    keys = jax.random.split(jax.random.key(seed), 3)
    blocks = normal_values(keys[0], (DIAGS, NBG, BS, BS), 0.05, 0.29882812, ((1, 8), (2, 4)))
    presence = draw_presence(jax.random.fold_in(keys[2], 71), 0)
    return {"blocks": blocks, "presence": presence}


def offset_table():
    values = list(range(-BAND, BAND + 1))
    values = values + [FAR - 1, FAR, FAR + 1, -FAR - 1, -FAR, -FAR + 1]
    return [value % NBG for value in values]


def pair_table(offsets):
    by_target = []
    for target_index in range(len(offsets)):
        entries = []
        for left_index in range(len(offsets)):
            for right_index in range(len(offsets)):
                if (offsets[left_index] + offsets[right_index]) % NBG == offsets[target_index]:
                    entries.append((left_index, right_index))
        by_target.append(entries)
    return by_target


def reference(blocks, presence):
    offsets = offset_table()
    by_target = pair_table(offsets)
    weight_mask = presence.astype(jnp.float32)[:, :, None, None]
    masked = blocks * presence.astype(jnp.bfloat16)[:, :, None, None]

    def product(left_tiles):
        totals = []
        for target_index in range(len(offsets)):
            total = jnp.zeros((NBG, BS, BS), jnp.float32)
            for left_index, right_index in by_target[target_index]:
                moved = jnp.roll(masked[right_index], -offsets[left_index], axis=0)
                total = total + jnp.einsum("ixz,izy->ixy", left_tiles[left_index].astype(jnp.float32), moved.astype(jnp.float32))
            totals.append(total)
        return jnp.stack(totals) * weight_mask

    second = product(masked).astype(jnp.bfloat16)
    third = product(second)
    return (3.0 * second.astype(jnp.float32) - 2.0 * third).astype(jnp.bfloat16)
```

```python
import functools
import math

import jax
import jax.numpy as jnp
from jax import lax
from jax.experimental import pallas as pl
from jax.experimental.pallas import tpu as pltpu
from jax.sharding import PartitionSpec as P

BAND = 3
FAR = 160
CHUNKS = 8
LAG = 2
WIDTH = 2 * BAND + 1
MESH = pl.DeviceIdType.MESH


def offset_table(total_rows):
    values = list(range(-BAND, BAND + 1))
    values = values + [FAR - 1, FAR, FAR + 1, -FAR - 1, -FAR, -FAR + 1]
    return [value % total_rows for value in values]


def pair_table(offsets, total_rows):
    by_target = []
    for target in offsets:
        entries = []
        for left_index, left in enumerate(offsets):
            for right_index, right in enumerate(offsets):
                if (left + right) % total_rows == target:
                    entries.append((left_index, right_index))
        by_target.append(entries)
    return by_target


def runs_of(indices):
    runs = []
    for position, index in enumerate(indices):
        if runs and runs[-1][1] + runs[-1][2] == index:
            runs[-1][2] += 1
        else:
            runs.append([position, index, 1])
    return runs


def pieces_of(low, high, local_rows):
    for ahead in range(low // local_rows, (high - 1) // local_rows + 1):
        first = max(low, ahead * local_rows)
        last = min(high, (ahead + 1) * local_rows)
        yield ahead, first - ahead * local_rows, last - first, first - low


def direct_kernel(sizes, needed, by_target, tiles, presence, out, near, ahead_far, behind_far, squared, done,
           send_sem, near_sem, ahead_sem, behind_sem, out_send_sem, out_sem):
    groups, columns, layers, local_rows, rows, part, size = sizes
    me_layer = lax.axis_index("layer")
    me_group = lax.axis_index("row") * columns + lax.axis_index("col")

    def device(steps, layer):
        group = lax.rem(me_group + steps % groups, groups)
        return {"row": lax.div(group, columns), "col": lax.rem(group, columns), "layer": layer}

    everything = list(range(len(by_target)))
    windows = [
        (near, near_sem, -BAND, 2 * BAND, everything),
        (ahead_far, ahead_sem, FAR - 1, 2, needed[0]),
        (behind_far, behind_sem, -FAR - 1, 2, needed[1]),
    ]
    chunks = CHUNKS if rows % CHUNKS == 0 else rows
    step_rows = rows // chunks

    def chunk_rows(chunk, extra):
        first = 0 if chunk == 0 else chunk * step_rows + extra
        return first, (chunk + 1) * step_rows + extra

    def copies_to(chunk, layer, act_remote, act_local):
        for window, sem, low, extra, diagonals in windows:
            first, last = chunk_rows(chunk, extra)
            start_row = low + layer * rows
            for steps, source_row, count, window_row in pieces_of(
                start_row + first, start_row + last, local_rows
            ):
                for position, index, length in runs_of(diagonals):
                    source = tiles.at[pl.ds(index, length), pl.ds(source_row, count)]
                    target = window.at[me_layer, pl.ds(position, length), pl.ds(first + window_row, count)]

                    def remote():
                        act_remote(
                            pltpu.make_async_remote_copy(
                                src_ref=source, dst_ref=target, send_sem=send_sem, recv_sem=sem.at[chunk],
                                device_id=device(-steps, layer), device_id_type=MESH,
                            )
                        )

                    def local():
                        if act_local is not None:
                            act_local(pltpu.make_async_copy(source, target, sem.at[chunk]))

                    if steps % groups == 0:
                        pl.when(me_layer != layer)(remote)
                        pl.when(me_layer == layer)(local)
                    else:
                        remote()

    def start(copy):
        copy.start()

    for chunk in range(chunks):
        for turn in range(layers):
            for layer in range(layers):

                @pl.when(lax.rem(me_layer + turn, layers) == layer)
                def _():
                    copies_to(chunk, layer, start, start)

    def wait_for(chunk):
        for window, sem, _, extra, _ in windows:
            first, last = chunk_rows(chunk, extra)
            arrived = window.at[:, :, pl.ds(first, last - first)]
            pltpu.make_async_copy(arrived, arrived, sem.at[chunk]).wait()

    def tile_of(window, index, row):
        return jnp.concatenate([window[layer, index, row] for layer in range(layers)], axis=0)

    def right_tile(left, right, row):
        if left < WIDTH:
            return tile_of(near, right, row + left)
        if left < WIDTH + 3:
            return tile_of(ahead_far, needed[0].index(right), row + left - WIDTH)
        return tile_of(behind_far, needed[1].index(right), row + left - WIDTH - 3)

    couples = [(0, 1), (2, 3), (4, 5), (6,), (7, 8), (9,), (10, 11), (12,)]

    def product(left_tile, row, finish):
        for couple in couples:
            tables = [dict(by_target[target]) for target in couple]
            lefts = sorted(set(left for table in tables for left in table))
            lhs = jnp.concatenate([left_tile(left) for left in lefts], axis=1)
            rhs = jnp.concatenate(
                [
                    jnp.concatenate(
                        [
                            right_tile(left, table[left], row)
                            if left in table
                            else jnp.zeros((size, size), jnp.bfloat16)
                            for table in tables
                        ],
                        axis=1,
                    )
                    for left in lefts
                ],
                axis=0,
            )
            total = jnp.dot(lhs, rhs, preferred_element_type=jnp.float32)
            for place, target in enumerate(couple):
                finish(target, total[:, place * size : (place + 1) * size])

    def each_result(row, act_remote, act_local):
        place = me_layer * rows + row
        for layer in range(layers):
            source = done.at[row, layer]
            target = out.at[:, place]

            def remote():
                act_remote(
                    pltpu.make_async_remote_copy(
                        src_ref=source, dst_ref=target, send_sem=out_send_sem, recv_sem=out_sem,
                        device_id=device(0, layer), device_id_type=MESH,
                    )
                )

            def local():
                if act_local is not None:
                    act_local(pltpu.make_async_copy(source, target, out_sem))

            pl.when(me_layer != layer)(remote)
            pl.when(me_layer == layer)(local)

    @pl.loop(0, rows)
    def _(row):
        for chunk in range(chunks):

            @pl.when(row == chunk * step_rows)
            def _():
                wait_for(chunk)

        def weight(target):
            return presence[target, me_layer * rows + row].astype(jnp.float32)

        def store_square(target, total):
            squared[target] = (total * weight(target)).astype(jnp.bfloat16)

        def store_result(target, total):
            third = total * weight(target)
            result = (3.0 * squared[target].astype(jnp.float32) - 2.0 * third).astype(jnp.bfloat16)
            for layer in range(layers):
                done[row, layer, target] = result[layer * part : (layer + 1) * part]

        product(lambda left: tile_of(near, left, row + BAND), row, store_square)
        product(lambda left: squared[left], row, store_result)

        @pl.when(row > 0)
        def _():
            each_result(row - 1, start, start)

    each_result(rows - 1, start, start)
    for chunk in range(chunks):
        for layer in range(layers):
            copies_to(chunk, layer, lambda copy: copy.wait_send(), None)

    @pl.loop(0, rows)
    def _(row):
        each_result(row, lambda copy: copy.wait_send(), None)

    pltpu.make_async_copy(out, out, out_sem).wait()


def relay_kernel(sizes, needed, by_target, tiles, presence, out, near, ahead, behind, squared, done,
                 send_sem, near_sem, near_edge_sem, far_band_sem, far_rest_sem, far_edge_sem, out_send_sem, out_sem):
    groups, columns, layers, local_rows, period, run, part, size = sizes
    steps = 2 * run
    distance = FAR // period
    band_first, band_count, rest_ahead, rest_behind = needed
    far_count = band_count + 3
    me_layer = lax.axis_index("layer")
    me_group = lax.axis_index("row") * columns + lax.axis_index("col")
    me_column = lax.axis_index("col")
    windows = (ahead, behind)

    def start(copy):
        copy.start()

    def wait_send(copy):
        copy.wait_send()

    def remote(source, target, sem, group, layer, act, sent=send_sem):
        group = lax.rem(group + 2 * groups, groups)
        act(
            pltpu.make_async_remote_copy(
                src_ref=source, dst_ref=target, send_sem=sent, recv_sem=sem,
                device_id={"row": lax.div(group, columns), "col": lax.rem(group, columns), "layer": layer},
                device_id_type=MESH,
            )
        )

    def arrived(view, sem):
        pltpu.make_async_copy(view, view, sem).wait()

    mine = pl.ds(pl.multiple_of(me_layer * part, part), part)

    def near_copies(half, place, first, count, sem, act, act_local):
        for turn in range(layers):
            layer = lax.rem(me_layer + turn, layers)
            row = half * period + layer * run + place - BAND
            ahead_groups = lax.div(row + local_rows, local_rows) - 1
            source = tiles.at[pl.ds(first, count), row - ahead_groups * local_rows]
            target = near.at[half, pl.ds(first, count), place, mine]

            def send():
                remote(source, target, sem, me_group - ahead_groups, layer, act)

            def local():
                if act_local is not None:
                    act_local(pltpu.make_async_copy(source, target, sem))

            if turn == 0:
                pl.when(ahead_groups != 0)(send)
                pl.when(ahead_groups == 0)(local)
            else:
                send()

    def edge_pieces(side):
        for position in range(BAND):
            place = position if side == 0 else run + BAND + position
            used = set()
            for pairs in by_target:
                for left, right in pairs:
                    if left < WIDTH and 0 <= place - left < run:
                        used.add(right)
            for piece, (_, first, count) in enumerate(runs_of(sorted(used))):
                yield side * BAND + position, place, piece, first, count

    def near_edges(side, act, act_local):
        for edge, place, piece, first, count in edge_pieces(side):
            for half in range(2):
                near_copies(half, place, first, count, near_edge_sem.at[half, edge, piece], act, act_local)

    def wait_near_edges(half, side):
        for edge, place, piece, first, count in edge_pieces(side):
            arrived(near.at[half, pl.ds(first, count), place], near_edge_sem.at[half, edge, piece])

    def row_of(step):
        return lax.rem(step + run - 1, run)

    def near_core(step, act, act_local):
        row = row_of(step)
        for half in range(2):
            near_copies(half, row + BAND, 0, len(by_target), near_sem.at[half, row], act, act_local)

    def each_near(act, act_local):
        @pl.loop(0, run)
        def _(step):
            near_core(step, act, act_local)

            @pl.when(step == 2)
            def _():
                near_edges(0, act, act_local)

        near_edges(1, act, act_local)

    def moves(phase):
        lower = (-distance // 2, (1 - distance) // 2)
        upper = (distance // 2, (1 + distance) // 2)
        return (
            jnp.where(phase == 0, lower[0], lower[1]),
            jnp.where(phase == 0, upper[0], upper[1]),
        )

    def relays(phase, column):
        down, up = moves(phase)
        column = lax.rem(column + 4 * groups, columns)
        first = lax.rem(column + down + 4 * groups, columns) - column
        second = lax.rem(column + up + 4 * groups, columns) - column
        alike = first * second > 0
        first, second = jnp.abs(first), jnp.abs(second)
        return alike & (first <= second), alike & (second < first)

    def far_sends(step, act):
        phase = lax.div(step, run)
        row = row_of(step)
        half = 1 - phase
        shifts = moves(phase)
        passes = relays(phase, me_column)
        band = near.at[phase, pl.ds(band_first, band_count), row + BAND]
        for side, rest in enumerate((rest_ahead, rest_behind)):
            group = me_group + shifts[side]

            @pl.when(jnp.logical_not(passes[1 - side]))
            def _():
                remote(band, windows[side].at[half, pl.ds(0, band_count), row + 1],
                       far_band_sem.at[side, half, row], group, me_layer, act)

            remote(near.at[phase, pl.ds(rest, 3), row + BAND],
                   windows[side].at[half, pl.ds(band_count, 3), row + 1],
                   far_rest_sem.at[side, half, row], group, me_layer, act)

    def far_relays(step, act, wait):
        phase = lax.div(step, run)
        row = row_of(step)
        half = 1 - phase
        shifts = moves(phase)
        passing = [relays(phase, me_column - shifts[side])[side] for side in range(2)]
        for side in range(2):

            @pl.when(passing[side])
            def _():
                view = windows[side].at[half, pl.ds(0, band_count), row + 1]
                if wait:
                    arrived(view, far_band_sem.at[side, half, row])
                remote(view, windows[1 - side].at[half, pl.ds(0, band_count), row + 1],
                       far_band_sem.at[1 - side, half, row],
                       me_group - shifts[side] + shifts[1 - side], me_layer, act)

        if wait:
            for side in range(2):

                @pl.when(jnp.logical_not(passing[side]))
                def _():
                    arrived(windows[side].at[half, pl.ds(0, band_count), row + 1], far_band_sem.at[side, half, row])

                arrived(windows[side].at[half, pl.ds(band_count, 3), row + 1], far_rest_sem.at[side, half, row])

    middle = band_count // 2
    left_edge = [(middle, far_count - middle)]
    right_edge = [(0, middle + 1), (band_count, 3)]

    def far_edges(step, act):
        half = 1 - lax.div(step, run)
        place = lax.rem(step, run)
        for which, pieces in enumerate((left_edge, right_edge)):

            @pl.when(place == which)
            def _():
                if which == 0:
                    over = me_layer == layers - 1
                    layer = jnp.where(over, 0, me_layer + 1)
                    window = half + jnp.where(over, 1, 0)
                else:
                    over = me_layer == 0
                    layer = jnp.where(over, layers - 1, me_layer - 1)
                    window = half - jnp.where(over, 1, 0)
                shift = lax.div(window + 2, 2) - 1
                target_half = window - 2 * shift
                source_row, target_row = (run, 0) if which == 0 else (1, run + 1)
                for side in range(2):
                    for piece, (first, count) in enumerate(pieces):
                        remote(windows[side].at[half, pl.ds(first, count), source_row],
                               windows[side].at[target_half, pl.ds(first, count), target_row],
                               far_edge_sem.at[side, target_half, which + piece],
                               me_group + shift, layer, act)

    def wait_far_edges(half, which):
        for side in range(2):
            for piece, (first, count) in enumerate((left_edge, right_edge)[which]):
                arrived(windows[side].at[half, pl.ds(first, count), 0 if which == 0 else run + 1],
                        far_edge_sem.at[side, half, which + piece])

    far_index = [
        list(range(band_first, band_first + band_count)) + list(range(rest, rest + 3))
        for rest in (rest_ahead, rest_behind)
    ]

    def right_tile(left, right, half, row):
        if left < WIDTH:
            return near[half, right, row + left]
        if left < WIDTH + 3:
            return ahead[half, far_index[0].index(right), row + left - WIDTH]
        return behind[half, far_index[1].index(right), row + left - WIDTH - 3]

    couples = [(0, 1), (2, 3), (4, 5), (6,), (7, 8), (9,), (10, 11), (12,)]

    def product(left_tile, half, row, finish):
        for couple in couples:
            tables = [dict(by_target[target]) for target in couple]
            lefts = sorted(set(left for table in tables for left in table))
            lhs = jnp.concatenate([left_tile(left) for left in lefts], axis=1)
            rhs = jnp.concatenate(
                [
                    jnp.concatenate(
                        [
                            right_tile(left, table[left], half, row)
                            if left in table
                            else jnp.zeros((size, size), jnp.bfloat16)
                            for table in tables
                        ],
                        axis=1,
                    )
                    for left in lefts
                ],
                axis=0,
            )
            total = jnp.dot(lhs, rhs, preferred_element_type=jnp.float32)
            for place, target in enumerate(couple):
                finish(target, total[:, place * size : (place + 1) * size])

    def row_at(position):
        inner = position < run - 2
        ends = jnp.logical_and(position >= run - 2, position < run)
        half = jnp.where(position < run, 1, 0)
        row = jnp.where(inner, position + 1, jnp.where(ends, (position - run + 2) * (run - 1), position - run))
        return half, row

    def computed_after(step):
        place = lax.rem(step, run)
        last = jnp.where(place == run - 1, 1, 0)
        early = jnp.where(place < 3, 0, place - 2) + last
        late = jnp.where(place < 2, run - 2, run + place - 1 + 2 * last)
        return jnp.where(step < 0, 0, jnp.where(step < run, early, late))

    def compute(position):
        half, row = row_at(position)
        for at, wait in (
            (0, lambda: wait_near_edges(1, 0)),
            (run - 4, lambda: wait_near_edges(1, 1)),
            (run - 2, lambda: wait_far_edges(1, 0)),
            (run - 1, lambda: wait_far_edges(1, 1)),
            (run, lambda: (wait_near_edges(0, 0), wait_far_edges(0, 0))),
            (2 * run - 3, lambda: wait_near_edges(0, 1)),
            (2 * run - 1, lambda: wait_far_edges(0, 1)),
        ):

            @pl.when(position == at)
            def _():
                wait()

        global_row = half * period + me_layer * run + row

        def weight(target):
            return presence[target, global_row].astype(jnp.float32)

        def store_square(target, total):
            squared[target] = (total * weight(target)).astype(jnp.bfloat16)

        def store_result(target, total):
            third = total * weight(target)
            result = (3.0 * squared[target].astype(jnp.float32) - 2.0 * third).astype(jnp.bfloat16)
            for layer in range(layers):
                done[position, layer, target] = result[layer * part : (layer + 1) * part]

        product(lambda left: near[half, left, row + BAND], half, row, store_square)
        product(lambda left: squared[left], half, row, store_result)

    def each_result(position, act, act_local):
        half, row = row_at(position)
        target = out.at[:, half * period + me_layer * run + row]
        for turn in range(layers):
            layer = lax.rem(me_layer + turn, layers)
            source = done.at[position, layer]
            if turn == 0:
                if act_local is not None:
                    act_local(pltpu.make_async_copy(source, target, out_sem))
            else:
                remote(source, target, out_sem, me_group, layer, act, out_send_sem)

    each_near(start, start)

    @pl.loop(0, steps + LAG)
    def _(step):
        @pl.when(step < run)
        def _():
            row = row_of(step)
            for half in range(2):
                arrived(near.at[half, :, row + BAND], near_sem.at[half, row])

        @pl.when(step < steps)
        def _():
            far_sends(step, start)

        @pl.when(step >= LAG)
        def _():
            settled = step - LAG
            far_relays(settled, start, True)
            far_edges(settled, start)

            @pl.loop(computed_after(settled - 1), computed_after(settled))
            def _(position):
                compute(position)

                @pl.when(position > 0)
                def _():
                    each_result(position - 1, start, start)

    each_result(steps - 1, start, start)
    each_near(wait_send, None)

    @pl.loop(0, steps)
    def _(step):
        far_sends(step, wait_send)
        far_relays(step, wait_send, False)
        far_edges(step, wait_send)
        each_result(step, wait_send, None)

    arrived(out, out_sem)


def relay_plan(groups, local_rows, layers, by_target):
    total_rows = groups * local_rows
    period = math.gcd(FAR, total_rows)
    if local_rows != 2 * period or period % layers or (FAR // period) % 2 == 0 or period // layers < 2 * BAND:
        return None
    by_side = []
    for first in (WIDTH, WIDTH + 3):
        lefts = range(first, first + 3)
        by_side.append(set(b for pairs in by_target for a, b in pairs if a in lefts))
    band = sorted(b for b in by_side[0] if b < WIDTH)
    wanted = [set(band) | set(range(WIDTH + 3, WIDTH + 6)), set(band) | set(range(WIDTH, WIDTH + 3))]
    if by_side != wanted or band != list(range(band[0], band[0] + len(band))):
        return None
    return period, period // layers, (band[0], len(band), WIDTH + 3, WIDTH)


def relay_call(sizes, needed, by_target, masked, presence):
    run, part, size = sizes[-3:]
    diagonals = masked.shape[0]
    layers = sizes[2]
    far = needed[1] + 3
    return pl.pallas_call(
        functools.partial(relay_kernel, sizes, needed, by_target),
        out_shape=jax.ShapeDtypeStruct(masked.shape, jnp.bfloat16),
        in_specs=[pl.BlockSpec(memory_space=pl.ANY), pl.BlockSpec(memory_space=pltpu.SMEM)],
        out_specs=pl.BlockSpec(memory_space=pl.ANY),
        scratch_shapes=[
            pltpu.VMEM((2, diagonals, run + 2 * BAND, size, size), jnp.bfloat16),
            pltpu.VMEM((2, far, run + 2, size, size), jnp.bfloat16),
            pltpu.VMEM((2, far, run + 2, size, size), jnp.bfloat16),
            pltpu.VMEM((diagonals, size, size), jnp.bfloat16),
            pltpu.VMEM((2 * run, layers, diagonals, part, size), jnp.bfloat16),
            pltpu.SemaphoreType.DMA,
            pltpu.SemaphoreType.DMA((2, run)),
            pltpu.SemaphoreType.DMA((2, 2 * BAND, 3)),
            pltpu.SemaphoreType.DMA((2, 2, run)),
            pltpu.SemaphoreType.DMA((2, 2, run)),
            pltpu.SemaphoreType.DMA((2, 2, 3)),
            pltpu.SemaphoreType.DMA,
            pltpu.SemaphoreType.DMA,
        ],
        compiler_params=pltpu.CompilerParams(has_side_effects=True, vmem_limit_bytes=52 * 2**20),
    )(masked, presence)


def solution(mesh):
    columns = mesh.shape["col"]
    layers = mesh.shape["layer"]
    groups = mesh.shape["row"] * columns

    def per_device(blocks, presence):
        diagonals, local_rows, part, size = blocks.shape
        total_rows = local_rows * groups
        rows = local_rows // layers
        offsets = offset_table(total_rows)
        by_target = pair_table(offsets, total_rows)
        plan = relay_plan(groups, local_rows, layers, by_target)
        masked = blocks * presence.astype(jnp.bfloat16)[:, :, None, None]
        if plan is not None:
            period, run, needed = plan
            sizes = (groups, columns, layers, local_rows, period, run, part, size)
            return relay_call(sizes, needed, by_target, masked, presence)
        needed = []
        for first in (WIDTH, WIDTH + 3):
            lefts = range(first, first + 3)
            needed.append(sorted(set(b for pairs in by_target for a, b in pairs if a in lefts)))
        sizes = (groups, columns, layers, local_rows, rows, part, size)
        return pl.pallas_call(
            functools.partial(direct_kernel, sizes, needed, by_target),
            out_shape=jax.ShapeDtypeStruct(blocks.shape, jnp.bfloat16),
            in_specs=[pl.BlockSpec(memory_space=pl.ANY), pl.BlockSpec(memory_space=pltpu.SMEM)],
            out_specs=pl.BlockSpec(memory_space=pl.ANY),
            scratch_shapes=[
                pltpu.VMEM((layers, diagonals, rows + 2 * BAND, part, size), jnp.bfloat16),
                pltpu.VMEM((layers, len(needed[0]), rows + 2, part, size), jnp.bfloat16),
                pltpu.VMEM((layers, len(needed[1]), rows + 2, part, size), jnp.bfloat16),
                pltpu.VMEM((diagonals, size, size), jnp.bfloat16),
                pltpu.VMEM((rows, layers, diagonals, part, size), jnp.bfloat16),
                pltpu.SemaphoreType.DMA,
                pltpu.SemaphoreType.DMA((rows,)),
                pltpu.SemaphoreType.DMA((rows,)),
                pltpu.SemaphoreType.DMA((rows,)),
                pltpu.SemaphoreType.DMA,
                pltpu.SemaphoreType.DMA,
            ],
            compiler_params=pltpu.CompilerParams(has_side_effects=True, vmem_limit_bytes=48 * 2**20),
        )(masked, presence)

    return jax.shard_map(
        per_device,
        mesh=mesh,
        in_specs=(P(None, ("row", "col"), "layer", None), P(None, ("row", "col"))),
        out_specs=P(None, ("row", "col"), "layer", None),
        check_vma=False,
    )
```

```python
import functools
import math

import jax
import jax.numpy as jnp
from jax import lax
from jax.experimental import pallas as pl
from jax.experimental.pallas import tpu as pltpu
from jax.sharding import PartitionSpec as P

BAND = 3
FAR = 160
CHUNKS = 8
RELAY_LAG = 2
LAG = 3
PACE = 1
WIDTH = 2 * BAND + 1
MESH = pl.DeviceIdType.MESH


def offset_table(total_rows):
    values = list(range(-BAND, BAND + 1))
    values = values + [FAR - 1, FAR, FAR + 1, -FAR - 1, -FAR, -FAR + 1]
    return [value % total_rows for value in values]


def pair_table(offsets, total_rows):
    by_target = []
    for target in offsets:
        entries = []
        for left_index, left in enumerate(offsets):
            for right_index, right in enumerate(offsets):
                if (left + right) % total_rows == target:
                    entries.append((left_index, right_index))
        by_target.append(entries)
    return by_target


def runs_of(indices):
    runs = []
    for position, index in enumerate(indices):
        if runs and runs[-1][1] + runs[-1][2] == index:
            runs[-1][2] += 1
        else:
            runs.append([position, index, 1])
    return runs


def pieces_of(low, high, local_rows):
    for ahead in range(low // local_rows, (high - 1) // local_rows + 1):
        first = max(low, ahead * local_rows)
        last = min(high, (ahead + 1) * local_rows)
        yield ahead, first - ahead * local_rows, last - first, first - low


def direct_kernel(sizes, needed, by_target, tiles, presence, out, near, ahead_far, behind_far, squared, done,
           send_sem, near_sem, ahead_sem, behind_sem, out_send_sem, out_sem):
    groups, columns, layers, local_rows, rows, part, size = sizes
    me_layer = lax.axis_index("layer")
    me_group = lax.axis_index("row") * columns + lax.axis_index("col")

    def device(steps, layer):
        group = lax.rem(me_group + steps % groups, groups)
        return {"row": lax.div(group, columns), "col": lax.rem(group, columns), "layer": layer}

    everything = list(range(len(by_target)))
    windows = [
        (near, near_sem, -BAND, 2 * BAND, everything),
        (ahead_far, ahead_sem, FAR - 1, 2, needed[0]),
        (behind_far, behind_sem, -FAR - 1, 2, needed[1]),
    ]
    chunks = CHUNKS if rows % CHUNKS == 0 else rows
    step_rows = rows // chunks

    def chunk_rows(chunk, extra):
        first = 0 if chunk == 0 else chunk * step_rows + extra
        return first, (chunk + 1) * step_rows + extra

    def copies_to(chunk, layer, act_remote, act_local):
        for window, sem, low, extra, diagonals in windows:
            first, last = chunk_rows(chunk, extra)
            start_row = low + layer * rows
            for steps, source_row, count, window_row in pieces_of(
                start_row + first, start_row + last, local_rows
            ):
                for position, index, length in runs_of(diagonals):
                    source = tiles.at[pl.ds(index, length), pl.ds(source_row, count)]
                    target = window.at[me_layer, pl.ds(position, length), pl.ds(first + window_row, count)]

                    def remote():
                        act_remote(
                            pltpu.make_async_remote_copy(
                                src_ref=source, dst_ref=target, send_sem=send_sem, recv_sem=sem.at[chunk],
                                device_id=device(-steps, layer), device_id_type=MESH,
                            )
                        )

                    def local():
                        if act_local is not None:
                            act_local(pltpu.make_async_copy(source, target, sem.at[chunk]))

                    if steps % groups == 0:
                        pl.when(me_layer != layer)(remote)
                        pl.when(me_layer == layer)(local)
                    else:
                        remote()

    def start(copy):
        copy.start()

    for chunk in range(chunks):
        for turn in range(layers):
            for layer in range(layers):

                @pl.when(lax.rem(me_layer + turn, layers) == layer)
                def _():
                    copies_to(chunk, layer, start, start)

    def wait_for(chunk):
        for window, sem, _, extra, _ in windows:
            first, last = chunk_rows(chunk, extra)
            arrived = window.at[:, :, pl.ds(first, last - first)]
            pltpu.make_async_copy(arrived, arrived, sem.at[chunk]).wait()

    def tile_of(window, index, row):
        return jnp.concatenate([window[layer, index, row] for layer in range(layers)], axis=0)

    def right_tile(left, right, row):
        if left < WIDTH:
            return tile_of(near, right, row + left)
        if left < WIDTH + 3:
            return tile_of(ahead_far, needed[0].index(right), row + left - WIDTH)
        return tile_of(behind_far, needed[1].index(right), row + left - WIDTH - 3)

    couples = [(0, 1), (2, 3), (4, 5), (6,), (7, 8), (9,), (10, 11), (12,)]

    def product(left_tile, row, finish):
        for couple in couples:
            tables = [dict(by_target[target]) for target in couple]
            lefts = sorted(set(left for table in tables for left in table))
            lhs = jnp.concatenate([left_tile(left) for left in lefts], axis=1)
            rhs = jnp.concatenate(
                [
                    jnp.concatenate(
                        [
                            right_tile(left, table[left], row)
                            if left in table
                            else jnp.zeros((size, size), jnp.bfloat16)
                            for table in tables
                        ],
                        axis=1,
                    )
                    for left in lefts
                ],
                axis=0,
            )
            total = jnp.dot(lhs, rhs, preferred_element_type=jnp.float32)
            for place, target in enumerate(couple):
                finish(target, total[:, place * size : (place + 1) * size])

    def each_result(row, act_remote, act_local):
        place = me_layer * rows + row
        for layer in range(layers):
            source = done.at[row, layer]
            target = out.at[:, place]

            def remote():
                act_remote(
                    pltpu.make_async_remote_copy(
                        src_ref=source, dst_ref=target, send_sem=out_send_sem, recv_sem=out_sem,
                        device_id=device(0, layer), device_id_type=MESH,
                    )
                )

            def local():
                if act_local is not None:
                    act_local(pltpu.make_async_copy(source, target, out_sem))

            pl.when(me_layer != layer)(remote)
            pl.when(me_layer == layer)(local)

    @pl.loop(0, rows)
    def _(row):
        for chunk in range(chunks):

            @pl.when(row == chunk * step_rows)
            def _():
                wait_for(chunk)

        def weight(target):
            return presence[target, me_layer * rows + row].astype(jnp.float32)

        def store_square(target, total):
            squared[target] = (total * weight(target)).astype(jnp.bfloat16)

        def store_result(target, total):
            third = total * weight(target)
            result = (3.0 * squared[target].astype(jnp.float32) - 2.0 * third).astype(jnp.bfloat16)
            for layer in range(layers):
                done[row, layer, target] = result[layer * part : (layer + 1) * part]

        product(lambda left: tile_of(near, left, row + BAND), row, store_square)
        product(lambda left: squared[left], row, store_result)

        @pl.when(row > 0)
        def _():
            each_result(row - 1, start, start)

    each_result(rows - 1, start, start)
    for chunk in range(chunks):
        for layer in range(layers):
            copies_to(chunk, layer, lambda copy: copy.wait_send(), None)

    @pl.loop(0, rows)
    def _(row):
        each_result(row, lambda copy: copy.wait_send(), None)

    pltpu.make_async_copy(out, out, out_sem).wait()


def relay_kernel(sizes, needed, by_target, blocks, presence, out, tiles, near, ahead, behind, squared, done,
                 load_sem, send_sem, near_sem, near_edge_sem, far_band_sem, far_rest_sem, far_edge_sem, out_send_sem, out_sem):
    groups, columns, layers, local_rows, period, run, part, size = sizes
    steps = 2 * run
    distance = FAR // period
    band_first, band_count, rest_ahead, rest_behind = needed
    far_count = band_count + 3
    me_layer = lax.axis_index("layer")
    me_group = lax.axis_index("row") * columns + lax.axis_index("col")
    me_column = lax.axis_index("col")
    windows = (ahead, behind)

    def start(copy):
        copy.start()

    def wait_send(copy):
        copy.wait_send()

    def remote(source, target, sem, group, layer, act, sent=send_sem):
        group = lax.rem(group + 2 * groups, groups)
        act(
            pltpu.make_async_remote_copy(
                src_ref=source, dst_ref=target, send_sem=sent, recv_sem=sem,
                device_id={"row": lax.div(group, columns), "col": lax.rem(group, columns), "layer": layer},
                device_id_type=MESH,
            )
        )

    def arrived(view, sem):
        pltpu.make_async_copy(view, view, sem).wait()

    mine = pl.ds(pl.multiple_of(me_layer * part, part), part)

    def near_copies(half, place, first, count, sem, act, act_local):
        for turn in range(layers):
            layer = lax.rem(me_layer + turn, layers)
            row = half * period + layer * run + place - BAND
            ahead_groups = lax.div(row + local_rows, local_rows) - 1
            source = tiles.at[pl.ds(first, count), row - ahead_groups * local_rows]
            target = near.at[half, pl.ds(first, count), place, mine]

            def send():
                remote(source, target, sem, me_group - ahead_groups, layer, act)

            def local():
                if act_local is not None:
                    act_local(pltpu.make_async_copy(source, target, sem))

            if turn == 0:
                pl.when(ahead_groups != 0)(send)
                pl.when(ahead_groups == 0)(local)
            else:
                send()

    def edge_pieces(side):
        for position in range(BAND):
            place = position if side == 0 else run + BAND + position
            used = set()
            for pairs in by_target:
                for left, right in pairs:
                    if left < WIDTH and 0 <= place - left < run:
                        used.add(right)
            for piece, (_, first, count) in enumerate(runs_of(sorted(used))):
                yield side * BAND + position, place, piece, first, count

    def near_edges(side, act, act_local):
        for edge, place, piece, first, count in edge_pieces(side):
            for half in range(2):
                near_copies(half, place, first, count, near_edge_sem.at[half, edge, piece], act, act_local)

    def wait_near_edges(half, side):
        for edge, place, piece, first, count in edge_pieces(side):
            arrived(near.at[half, pl.ds(first, count), place], near_edge_sem.at[half, edge, piece])

    def row_of(step):
        return lax.rem(step + run - 1, run)

    def near_step(step, act, act_local):
        half = lax.div(step, run)
        row = row_of(step)
        near_copies(half, row + BAND, 0, len(by_target), near_sem.at[half, row], act, act_local)

    def own_row(step, layer):
        return lax.div(step, run) * period + layer * run + row_of(step)

    def loads(step, act):
        for layer in range(layers):
            row = own_row(step, layer)
            act(pltpu.make_async_copy(blocks.at[:, row], tiles.at[:, row], load_sem.at[step, layer]))

    def mask(step):
        for layer in range(layers):
            row = own_row(step, layer)
            for target in range(len(by_target)):
                weight = presence[target, row].astype(jnp.float32)
                tiles[target, row] = (tiles[target, row].astype(jnp.float32) * weight).astype(jnp.bfloat16)

    def send_near():
        @pl.loop(0, steps)
        def _(step):
            loads(step, start)

        @pl.loop(0, steps + 1)
        def _(step):
            @pl.when(step < steps)
            def _():
                loads(step, lambda copy: copy.wait())
                mask(step)

            @pl.when(step > 0)
            def _():
                near_step(step - 1, start, start)

        for side in range(2):
            near_edges(side, start, start)

    def wait_near_sends():
        @pl.loop(0, steps)
        def _(step):
            near_step(step, wait_send, None)

        for side in range(2):
            near_edges(side, wait_send, None)

    def wait_near(half, row):
        arrived(near.at[half, :, row + BAND], near_sem.at[half, row])

    def moves(phase):
        lower = (-distance // 2, (1 - distance) // 2)
        upper = (distance // 2, (1 + distance) // 2)
        return (
            jnp.where(phase == 0, lower[0], lower[1]),
            jnp.where(phase == 0, upper[0], upper[1]),
        )

    def relays(phase, column):
        down, up = moves(phase)
        column = lax.rem(column + 4 * groups, columns)
        first = lax.rem(column + down + 4 * groups, columns) - column
        second = lax.rem(column + up + 4 * groups, columns) - column
        alike = first * second > 0
        middle = columns // 2

        def crosses(shift):
            return (column < middle) != (column + shift < middle)

        nearer = jnp.abs(first) <= jnp.abs(second)
        return (
            alike & nearer & crosses(first),
            alike & jnp.logical_not(nearer) & crosses(second),
        )

    def far_sends(step, act):
        phase = lax.div(step, run)
        row = row_of(step)
        half = 1 - phase
        shifts = moves(phase)
        passes = relays(phase, me_column)
        band = near.at[phase, pl.ds(band_first, band_count), row + BAND]
        for side, rest in enumerate((rest_ahead, rest_behind)):
            group = me_group + shifts[side]

            @pl.when(jnp.logical_not(passes[1 - side]))
            def _():
                remote(band, windows[side].at[half, pl.ds(0, band_count), row + 1],
                       far_band_sem.at[side, half, row], group, me_layer, act)

            remote(near.at[phase, pl.ds(rest, 3), row + BAND],
                   windows[side].at[half, pl.ds(band_count, 3), row + 1],
                   far_rest_sem.at[side, half, row], group, me_layer, act)

    def passes_on(phase):
        shifts = moves(phase)
        return [relays(phase, me_column - shifts[side])[side] for side in range(2)]

    def far_relays(step, act, wait):
        phase = lax.div(step, run)
        row = row_of(step)
        half = 1 - phase
        shifts = moves(phase)
        for side, passing in enumerate(passes_on(phase)):

            @pl.when(passing)
            def _():
                view = windows[side].at[half, pl.ds(0, band_count), row + 1]
                if wait:
                    arrived(view, far_band_sem.at[side, half, row])
                remote(view, windows[1 - side].at[half, pl.ds(0, band_count), row + 1],
                       far_band_sem.at[1 - side, half, row],
                       me_group - shifts[side] + shifts[1 - side], me_layer, act)

    def wait_far(step):
        phase = lax.div(step, run)
        row = row_of(step)
        half = 1 - phase
        for side, passing in enumerate(passes_on(phase)):

            @pl.when(jnp.logical_not(passing))
            def _():
                arrived(windows[side].at[half, pl.ds(0, band_count), row + 1], far_band_sem.at[side, half, row])

            arrived(windows[side].at[half, pl.ds(band_count, 3), row + 1], far_rest_sem.at[side, half, row])

    middle = band_count // 2
    left_edge = [(middle, far_count - middle)]
    right_edge = [(0, middle + 1), (band_count, 3)]

    def far_edges(step, act):
        half = 1 - lax.div(step, run)
        place = lax.rem(step, run)
        for which, pieces in enumerate((left_edge, right_edge)):

            @pl.when(place == which)
            def _():
                if which == 0:
                    over = me_layer == layers - 1
                    layer = jnp.where(over, 0, me_layer + 1)
                    window = half + jnp.where(over, 1, 0)
                else:
                    over = me_layer == 0
                    layer = jnp.where(over, layers - 1, me_layer - 1)
                    window = half - jnp.where(over, 1, 0)
                shift = lax.div(window + 2, 2) - 1
                target_half = window - 2 * shift
                source_row, target_row = (run, 0) if which == 0 else (1, run + 1)
                for side in range(2):
                    for piece, (first, count) in enumerate(pieces):
                        remote(windows[side].at[half, pl.ds(first, count), source_row],
                               windows[side].at[target_half, pl.ds(first, count), target_row],
                               far_edge_sem.at[side, target_half, which + piece],
                               me_group + shift, layer, act)

    def wait_far_edges(half, which):
        for side in range(2):
            for piece, (first, count) in enumerate((left_edge, right_edge)[which]):
                arrived(windows[side].at[half, pl.ds(first, count), 0 if which == 0 else run + 1],
                        far_edge_sem.at[side, half, which + piece])

    far_index = [
        list(range(band_first, band_first + band_count)) + list(range(rest, rest + 3))
        for rest in (rest_ahead, rest_behind)
    ]

    def right_tile(left, right, half, row):
        if left < WIDTH:
            return near[half, right, row + left]
        if left < WIDTH + 3:
            return ahead[half, far_index[0].index(right), row + left - WIDTH]
        return behind[half, far_index[1].index(right), row + left - WIDTH - 3]

    couples = [(0, 1), (2, 3), (4, 5), (6,), (7, 8), (9,), (10, 11), (12,)]

    def product(left_tile, half, row, finish):
        for couple in couples:
            tables = [dict(by_target[target]) for target in couple]
            lefts = sorted(set(left for table in tables for left in table))
            lhs = jnp.concatenate([left_tile(left) for left in lefts], axis=1)
            rhs = jnp.concatenate(
                [
                    jnp.concatenate(
                        [
                            right_tile(left, table[left], half, row)
                            if left in table
                            else jnp.zeros((size, size), jnp.bfloat16)
                            for table in tables
                        ],
                        axis=1,
                    )
                    for left in lefts
                ],
                axis=0,
            )
            total = jnp.dot(lhs, rhs, preferred_element_type=jnp.float32)
            for place, target in enumerate(couple):
                finish(target, total[:, place * size : (place + 1) * size])

    def row_at(position):
        inner = position < run - 2
        half = jnp.where(position < run, 1, 0)
        ends = jnp.where(position < run, (position - run + 2) * (run - 1), position - run)
        return half, jnp.where(inner, position + 1, ends)

    def computed_after(step):
        since = step - run
        early = jnp.where(since < 3, jnp.maximum(since, 0), jnp.minimum(2 * since - 2, run - 2))
        place = step - LAG - run
        late = jnp.where(place < 2, run - 1, run + place - 1)
        late = jnp.where(place >= run - 1, steps, late)
        return jnp.where(place < 1, early, late)

    def compute(position):
        half, row = row_at(position)
        for at_half, at_row, wait in (
            (1, 1, lambda: wait_near_edges(1, 0)),
            (1, run - BAND, lambda: wait_near_edges(1, 1)),
            (1, 0, lambda: wait_far_edges(1, 0)),
            (1, run - 1, lambda: wait_far_edges(1, 1)),
            (0, 0, lambda: (wait_near_edges(0, 0), wait_far_edges(0, 0))),
            (0, run - BAND, lambda: wait_near_edges(0, 1)),
            (0, run - 1, lambda: wait_far_edges(0, 1)),
        ):

            @pl.when(jnp.logical_and(half == at_half, row == at_row))
            def _():
                wait()

        global_row = half * period + me_layer * run + row

        def weight(target):
            return presence[target, global_row].astype(jnp.float32)

        def store_square(target, total):
            squared[target] = (total * weight(target)).astype(jnp.bfloat16)

        def store_result(target, total):
            third = total * weight(target)
            result = (3.0 * squared[target].astype(jnp.float32) - 2.0 * third).astype(jnp.bfloat16)
            for layer in range(layers):
                done[position, layer, target] = result[layer * part : (layer + 1) * part]

        product(lambda left: near[half, left, row + BAND], half, row, store_square)
        product(lambda left: squared[left], half, row, store_result)

    def each_result(position, act, act_local):
        half, row = row_at(position)
        target = out.at[:, half * period + me_layer * run + row]
        for turn in range(layers):
            layer = lax.rem(me_layer + turn, layers)
            source = done.at[position, layer]
            if turn == 0:
                if act_local is not None:
                    act_local(pltpu.make_async_copy(source, target, out_sem))
            else:
                remote(source, target, out_sem, me_group, layer, act, out_send_sem)

    send_near()

    @pl.loop(0, steps + LAG)
    def _(step):
        other = step - run // 2

        @pl.when(jnp.logical_and(other >= 0, other < run))
        def _():
            wait_near(1, row_of(other))

        @pl.loop(jnp.minimum(PACE * step, steps), jnp.minimum(PACE * (step + 1), steps))
        def _(sent):
            @pl.when(sent < run)
            def _():
                wait_near(0, row_of(sent))

            far_sends(sent, start)

        @pl.when(jnp.logical_and(step >= RELAY_LAG, step < steps + RELAY_LAG))
        def _():
            far_relays(step - RELAY_LAG, start, True)

        @pl.when(step >= LAG)
        def _():
            settled = step - LAG
            wait_far(settled)
            far_edges(settled, start)

            @pl.loop(computed_after(step - 1), computed_after(step))
            def _(position):
                compute(position)

                @pl.when(position > 0)
                def _():
                    each_result(position - 1, start, start)

    each_result(steps - 1, start, start)
    wait_near_sends()

    @pl.loop(0, steps)
    def _(step):
        far_sends(step, wait_send)
        far_relays(step, wait_send, False)
        far_edges(step, wait_send)
        each_result(step, wait_send, None)

    arrived(out, out_sem)


def relay_plan(groups, local_rows, layers, by_target):
    total_rows = groups * local_rows
    period = math.gcd(FAR, total_rows)
    if local_rows != 2 * period or period % layers or (FAR // period) % 2 == 0 or period // layers < 2 * BAND + 2:
        return None
    by_side = []
    for first in (WIDTH, WIDTH + 3):
        lefts = range(first, first + 3)
        by_side.append(set(b for pairs in by_target for a, b in pairs if a in lefts))
    band = sorted(b for b in by_side[0] if b < WIDTH)
    wanted = [set(band) | set(range(WIDTH + 3, WIDTH + 6)), set(band) | set(range(WIDTH, WIDTH + 3))]
    if by_side != wanted or band != list(range(band[0], band[0] + len(band))):
        return None
    return period, period // layers, (band[0], len(band), WIDTH + 3, WIDTH)


def relay_call(sizes, needed, by_target, blocks, presence):
    run, part, size = sizes[-3:]
    diagonals = blocks.shape[0]
    layers = sizes[2]
    far = needed[1] + 3
    return pl.pallas_call(
        functools.partial(relay_kernel, sizes, needed, by_target),
        out_shape=jax.ShapeDtypeStruct(blocks.shape, jnp.bfloat16),
        in_specs=[pl.BlockSpec(memory_space=pl.ANY), pl.BlockSpec(memory_space=pltpu.SMEM)],
        out_specs=pl.BlockSpec(memory_space=pl.ANY),
        scratch_shapes=[
            pltpu.VMEM(blocks.shape, jnp.bfloat16),
            pltpu.VMEM((2, diagonals, run + 2 * BAND, size, size), jnp.bfloat16),
            pltpu.VMEM((2, far, run + 2, size, size), jnp.bfloat16),
            pltpu.VMEM((2, far, run + 2, size, size), jnp.bfloat16),
            pltpu.VMEM((diagonals, size, size), jnp.bfloat16),
            pltpu.VMEM((2 * run, layers, diagonals, part, size), jnp.bfloat16),
            pltpu.SemaphoreType.DMA((2 * run, layers)),
            pltpu.SemaphoreType.DMA,
            pltpu.SemaphoreType.DMA((2, run)),
            pltpu.SemaphoreType.DMA((2, 2 * BAND, 3)),
            pltpu.SemaphoreType.DMA((2, 2, run)),
            pltpu.SemaphoreType.DMA((2, 2, run)),
            pltpu.SemaphoreType.DMA((2, 2, 3)),
            pltpu.SemaphoreType.DMA,
            pltpu.SemaphoreType.DMA,
        ],
        compiler_params=pltpu.CompilerParams(has_side_effects=True, vmem_limit_bytes=52 * 2**20),
    )(blocks, presence)


def solution(mesh):
    columns = mesh.shape["col"]
    layers = mesh.shape["layer"]
    groups = mesh.shape["row"] * columns

    def per_device(blocks, presence):
        diagonals, local_rows, part, size = blocks.shape
        total_rows = local_rows * groups
        rows = local_rows // layers
        offsets = offset_table(total_rows)
        by_target = pair_table(offsets, total_rows)
        plan = relay_plan(groups, local_rows, layers, by_target)
        if plan is not None:
            period, run, needed = plan
            sizes = (groups, columns, layers, local_rows, period, run, part, size)
            return relay_call(sizes, needed, by_target, blocks, presence)
        needed = []
        for first in (WIDTH, WIDTH + 3):
            lefts = range(first, first + 3)
            needed.append(sorted(set(b for pairs in by_target for a, b in pairs if a in lefts)))
        masked = blocks * presence.astype(jnp.bfloat16)[:, :, None, None]
        sizes = (groups, columns, layers, local_rows, rows, part, size)
        return pl.pallas_call(
            functools.partial(direct_kernel, sizes, needed, by_target),
            out_shape=jax.ShapeDtypeStruct(blocks.shape, jnp.bfloat16),
            in_specs=[pl.BlockSpec(memory_space=pl.ANY), pl.BlockSpec(memory_space=pltpu.SMEM)],
            out_specs=pl.BlockSpec(memory_space=pl.ANY),
            scratch_shapes=[
                pltpu.VMEM((layers, diagonals, rows + 2 * BAND, part, size), jnp.bfloat16),
                pltpu.VMEM((layers, len(needed[0]), rows + 2, part, size), jnp.bfloat16),
                pltpu.VMEM((layers, len(needed[1]), rows + 2, part, size), jnp.bfloat16),
                pltpu.VMEM((diagonals, size, size), jnp.bfloat16),
                pltpu.VMEM((rows, layers, diagonals, part, size), jnp.bfloat16),
                pltpu.SemaphoreType.DMA,
                pltpu.SemaphoreType.DMA((rows,)),
                pltpu.SemaphoreType.DMA((rows,)),
                pltpu.SemaphoreType.DMA((rows,)),
                pltpu.SemaphoreType.DMA,
                pltpu.SemaphoreType.DMA,
            ],
            compiler_params=pltpu.CompilerParams(has_side_effects=True, vmem_limit_bytes=48 * 2**20),
        )(masked, presence)

    return jax.shard_map(
        per_device,
        mesh=mesh,
        in_specs=(P(None, ("row", "col"), "layer", None), P(None, ("row", "col"))),
        out_specs=P(None, ("row", "col"), "layer", None),
        check_vma=False,
    )
```

```python
import functools
import math

import jax
import jax.numpy as jnp
from jax import lax
from jax.experimental import pallas as pl
from jax.experimental.pallas import tpu as pltpu
from jax.sharding import PartitionSpec as P

BAND = 3
FAR = 160
CHUNKS = 8
RELAY_LAG = 2
LAG = 2
DIRECT = 1
FIRST = 16
RATE = 1
WIDTH = 2 * BAND + 1
MESH = pl.DeviceIdType.MESH


def offset_table(total_rows):
    values = list(range(-BAND, BAND + 1))
    values = values + [FAR - 1, FAR, FAR + 1, -FAR - 1, -FAR, -FAR + 1]
    return [value % total_rows for value in values]


def pair_table(offsets, total_rows):
    by_target = []
    for target in offsets:
        entries = []
        for left_index, left in enumerate(offsets):
            for right_index, right in enumerate(offsets):
                if (left + right) % total_rows == target:
                    entries.append((left_index, right_index))
        by_target.append(entries)
    return by_target


def runs_of(indices):
    runs = []
    for position, index in enumerate(indices):
        if runs and runs[-1][1] + runs[-1][2] == index:
            runs[-1][2] += 1
        else:
            runs.append([position, index, 1])
    return runs


def pieces_of(low, high, local_rows):
    for ahead in range(low // local_rows, (high - 1) // local_rows + 1):
        first = max(low, ahead * local_rows)
        last = min(high, (ahead + 1) * local_rows)
        yield ahead, first - ahead * local_rows, last - first, first - low


def direct_kernel(sizes, needed, by_target, tiles, presence, out, near, ahead_far, behind_far, squared, done,
           send_sem, near_sem, ahead_sem, behind_sem, out_send_sem, out_sem):
    groups, columns, layers, local_rows, rows, part, size = sizes
    me_layer = lax.axis_index("layer")
    me_group = lax.axis_index("row") * columns + lax.axis_index("col")

    def device(steps, layer):
        group = lax.rem(me_group + steps % groups, groups)
        return {"row": lax.div(group, columns), "col": lax.rem(group, columns), "layer": layer}

    everything = list(range(len(by_target)))
    windows = [
        (near, near_sem, -BAND, 2 * BAND, everything),
        (ahead_far, ahead_sem, FAR - 1, 2, needed[0]),
        (behind_far, behind_sem, -FAR - 1, 2, needed[1]),
    ]
    chunks = CHUNKS if rows % CHUNKS == 0 else rows
    step_rows = rows // chunks

    def chunk_rows(chunk, extra):
        first = 0 if chunk == 0 else chunk * step_rows + extra
        return first, (chunk + 1) * step_rows + extra

    def copies_to(chunk, layer, act_remote, act_local):
        for window, sem, low, extra, diagonals in windows:
            first, last = chunk_rows(chunk, extra)
            start_row = low + layer * rows
            for steps, source_row, count, window_row in pieces_of(
                start_row + first, start_row + last, local_rows
            ):
                for position, index, length in runs_of(diagonals):
                    source = tiles.at[pl.ds(index, length), pl.ds(source_row, count)]
                    target = window.at[me_layer, pl.ds(position, length), pl.ds(first + window_row, count)]

                    def remote():
                        act_remote(
                            pltpu.make_async_remote_copy(
                                src_ref=source, dst_ref=target, send_sem=send_sem, recv_sem=sem.at[chunk],
                                device_id=device(-steps, layer), device_id_type=MESH,
                            )
                        )

                    def local():
                        if act_local is not None:
                            act_local(pltpu.make_async_copy(source, target, sem.at[chunk]))

                    if steps % groups == 0:
                        pl.when(me_layer != layer)(remote)
                        pl.when(me_layer == layer)(local)
                    else:
                        remote()

    def start(copy):
        copy.start()

    for chunk in range(chunks):
        for turn in range(layers):
            for layer in range(layers):

                @pl.when(lax.rem(me_layer + turn, layers) == layer)
                def _():
                    copies_to(chunk, layer, start, start)

    def wait_for(chunk):
        for window, sem, _, extra, _ in windows:
            first, last = chunk_rows(chunk, extra)
            arrived = window.at[:, :, pl.ds(first, last - first)]
            pltpu.make_async_copy(arrived, arrived, sem.at[chunk]).wait()

    def tile_of(window, index, row):
        return jnp.concatenate([window[layer, index, row] for layer in range(layers)], axis=0)

    def right_tile(left, right, row):
        if left < WIDTH:
            return tile_of(near, right, row + left)
        if left < WIDTH + 3:
            return tile_of(ahead_far, needed[0].index(right), row + left - WIDTH)
        return tile_of(behind_far, needed[1].index(right), row + left - WIDTH - 3)

    couples = [(0, 1), (2, 3), (4, 5), (6,), (7, 8), (9,), (10, 11), (12,)]

    def product(left_tile, row, finish):
        for couple in couples:
            tables = [dict(by_target[target]) for target in couple]
            lefts = sorted(set(left for table in tables for left in table))
            lhs = jnp.concatenate([left_tile(left) for left in lefts], axis=1)
            rhs = jnp.concatenate(
                [
                    jnp.concatenate(
                        [
                            right_tile(left, table[left], row)
                            if left in table
                            else jnp.zeros((size, size), jnp.bfloat16)
                            for table in tables
                        ],
                        axis=1,
                    )
                    for left in lefts
                ],
                axis=0,
            )
            total = jnp.dot(lhs, rhs, preferred_element_type=jnp.float32)
            for place, target in enumerate(couple):
                finish(target, total[:, place * size : (place + 1) * size])

    def each_result(row, act_remote, act_local):
        place = me_layer * rows + row
        for layer in range(layers):
            source = done.at[row, layer]
            target = out.at[:, place]

            def remote():
                act_remote(
                    pltpu.make_async_remote_copy(
                        src_ref=source, dst_ref=target, send_sem=out_send_sem, recv_sem=out_sem,
                        device_id=device(0, layer), device_id_type=MESH,
                    )
                )

            def local():
                if act_local is not None:
                    act_local(pltpu.make_async_copy(source, target, out_sem))

            pl.when(me_layer != layer)(remote)
            pl.when(me_layer == layer)(local)

    @pl.loop(0, rows)
    def _(row):
        for chunk in range(chunks):

            @pl.when(row == chunk * step_rows)
            def _():
                wait_for(chunk)

        def weight(target):
            return presence[target, me_layer * rows + row].astype(jnp.float32)

        def store_square(target, total):
            squared[target] = (total * weight(target)).astype(jnp.bfloat16)

        def store_result(target, total):
            third = total * weight(target)
            result = (3.0 * squared[target].astype(jnp.float32) - 2.0 * third).astype(jnp.bfloat16)
            for layer in range(layers):
                done[row, layer, target] = result[layer * part : (layer + 1) * part]

        product(lambda left: tile_of(near, left, row + BAND), row, store_square)
        product(lambda left: squared[left], row, store_result)

        @pl.when(row > 0)
        def _():
            each_result(row - 1, start, start)

    each_result(rows - 1, start, start)
    for chunk in range(chunks):
        for layer in range(layers):
            copies_to(chunk, layer, lambda copy: copy.wait_send(), None)

    @pl.loop(0, rows)
    def _(row):
        each_result(row, lambda copy: copy.wait_send(), None)

    pltpu.make_async_copy(out, out, out_sem).wait()


def relay_kernel(sizes, needed, by_target, blocks, presence, out, tiles, near, ahead, behind, squared, done,
                 load_sem, send_sem, near_sem, near_edge_sem, far_band_sem, far_rest_sem, far_edge_sem, out_send_sem, out_sem):
    groups, columns, layers, local_rows, period, run, part, size = sizes
    steps = 2 * run
    distance = FAR // period
    band_first, band_count, rest_ahead, rest_behind = needed
    far_count = band_count + 3
    me_layer = lax.axis_index("layer")
    me_group = lax.axis_index("row") * columns + lax.axis_index("col")
    me_column = lax.axis_index("col")
    windows = (ahead, behind)

    def start(copy):
        copy.start()

    def wait_send(copy):
        copy.wait_send()

    def remote(source, target, sem, group, layer, act, sent=send_sem):
        group = lax.rem(group + 2 * groups, groups)
        act(
            pltpu.make_async_remote_copy(
                src_ref=source, dst_ref=target, send_sem=sent, recv_sem=sem,
                device_id={"row": lax.div(group, columns), "col": lax.rem(group, columns), "layer": layer},
                device_id_type=MESH,
            )
        )

    def arrived(view, sem):
        pltpu.make_async_copy(view, view, sem).wait()

    mine = pl.ds(pl.multiple_of(me_layer * part, part), part)

    def near_copies(half, place, first, count, sem, act, act_local):
        for turn in range(layers):
            layer = lax.rem(me_layer + turn, layers)
            row = half * period + layer * run + place - BAND
            ahead_groups = lax.div(row + local_rows, local_rows) - 1
            source = tiles.at[pl.ds(first, count), row - ahead_groups * local_rows]
            target = near.at[half, pl.ds(first, count), place, mine]

            def send():
                remote(source, target, sem, me_group - ahead_groups, layer, act)

            def local():
                if act_local is not None:
                    act_local(pltpu.make_async_copy(source, target, sem))

            if turn == 0:
                pl.when(ahead_groups != 0)(send)
                pl.when(ahead_groups == 0)(local)
            else:
                send()

    def edge_pieces(side):
        for position in range(BAND):
            place = position if side == 0 else run + BAND + position
            used = set()
            for pairs in by_target:
                for left, right in pairs:
                    if left < WIDTH and 0 <= place - left < run:
                        used.add(right)
            for piece, (_, first, count) in enumerate(runs_of(sorted(used))):
                yield side * BAND + position, place, piece, first, count

    def near_edges(side, act, act_local):
        for edge, place, piece, first, count in edge_pieces(side):
            for half in range(2):
                near_copies(half, place, first, count, near_edge_sem.at[half, edge, piece], act, act_local)

    def wait_near_edges(half, side):
        for edge, place, piece, first, count in edge_pieces(side):
            arrived(near.at[half, pl.ds(first, count), place], near_edge_sem.at[half, edge, piece])

    def row_of(step):
        return lax.rem(step + run - 1, run)

    def near_step(step, act, act_local):
        half = lax.div(step, run)
        row = row_of(step)
        near_copies(half, row + BAND, 0, len(by_target), near_sem.at[half, row], act, act_local)

    def own_row(step, layer):
        return lax.div(step, run) * period + layer * run + row_of(step)

    def loads(step, act):
        for layer in range(layers):
            row = own_row(step, layer)
            act(pltpu.make_async_copy(blocks.at[:, row], tiles.at[:, row], load_sem.at[step, layer]))

    def mask(step):
        for layer in range(layers):
            row = own_row(step, layer)
            for target in range(len(by_target)):
                weight = presence[target, row].astype(jnp.float32)
                tiles[target, row] = (tiles[target, row].astype(jnp.float32) * weight).astype(jnp.bfloat16)

    def prepare(step):
        @pl.when(step < steps)
        def _():
            loads(step, lambda copy: copy.wait())
            mask(step)

    def send_near(first, last):
        @pl.loop(first, last)
        def _(step):
            prepare(step + 2)
            near_step(step, start, start)

    def wait_near_sends():
        @pl.loop(0, steps)
        def _(step):
            near_step(step, wait_send, None)

        for side in range(2):
            near_edges(side, wait_send, None)

    def wait_near(half, row):
        arrived(near.at[half, :, row + BAND], near_sem.at[half, row])

    def moves(phase):
        lower = (-distance // 2, (1 - distance) // 2)
        upper = (distance // 2, (1 + distance) // 2)
        return (
            jnp.where(phase == 0, lower[0], lower[1]),
            jnp.where(phase == 0, upper[0], upper[1]),
        )

    def relays(phase, column):
        down, up = moves(phase)
        column = lax.rem(column + 4 * groups, columns)
        first = lax.rem(column + down + 4 * groups, columns) - column
        second = lax.rem(column + up + 4 * groups, columns) - column
        alike = first * second > 0
        middle = columns // 2

        def crosses(shift):
            return (column < middle) != (column + shift < middle)

        nearer = jnp.abs(first) <= jnp.abs(second)
        return (
            alike & nearer & crosses(first),
            alike & jnp.logical_not(nearer) & crosses(second),
        )

    def far_sends(step, act):
        phase = lax.div(step, run)
        row = row_of(step)
        half = 1 - phase
        shifts = moves(phase)
        passes = relays(phase, me_column)

        def send(side, first, count, place, sem):
            group = me_group + shifts[side]

            @pl.when(step < DIRECT)
            def _():
                for turn in range(layers):
                    layer = lax.rem(me_layer + turn, layers)
                    remote(tiles.at[pl.ds(first, count), own_row(step, layer)],
                           windows[side].at[half, pl.ds(place, count), row + 1, mine],
                           sem, group, layer, act)

            @pl.when(step >= DIRECT)
            def _():
                remote(near.at[phase, pl.ds(first, count), row + BAND],
                       windows[side].at[half, pl.ds(place, count), row + 1],
                       sem, group, me_layer, act)

        for side, rest in enumerate((rest_ahead, rest_behind)):

            @pl.when(jnp.logical_not(passes[1 - side]))
            def _():
                send(side, band_first, band_count, 0, far_band_sem.at[side, half, row])

            send(side, rest, 3, band_count, far_rest_sem.at[side, half, row])

    def passes_on(phase):
        shifts = moves(phase)
        return [relays(phase, me_column - shifts[side])[side] for side in range(2)]

    def far_relays(step, act, wait):
        phase = lax.div(step, run)
        row = row_of(step)
        half = 1 - phase
        shifts = moves(phase)
        for side, passing in enumerate(passes_on(phase)):

            @pl.when(passing)
            def _():
                view = windows[side].at[half, pl.ds(0, band_count), row + 1]
                if wait:
                    arrived(view, far_band_sem.at[side, half, row])
                remote(view, windows[1 - side].at[half, pl.ds(0, band_count), row + 1],
                       far_band_sem.at[1 - side, half, row],
                       me_group - shifts[side] + shifts[1 - side], me_layer, act)

    def wait_far(step):
        phase = lax.div(step, run)
        row = row_of(step)
        half = 1 - phase
        for side, passing in enumerate(passes_on(phase)):

            @pl.when(jnp.logical_not(passing))
            def _():
                arrived(windows[side].at[half, pl.ds(0, band_count), row + 1], far_band_sem.at[side, half, row])

            arrived(windows[side].at[half, pl.ds(band_count, 3), row + 1], far_rest_sem.at[side, half, row])

    middle = band_count // 2
    left_edge = [(middle, far_count - middle)]
    right_edge = [(0, middle + 1), (band_count, 3)]

    def far_edges(step, act):
        half = 1 - lax.div(step, run)
        place = lax.rem(step, run)
        for which, pieces in enumerate((left_edge, right_edge)):

            @pl.when(place == which)
            def _():
                if which == 0:
                    over = me_layer == layers - 1
                    layer = jnp.where(over, 0, me_layer + 1)
                    window = half + jnp.where(over, 1, 0)
                else:
                    over = me_layer == 0
                    layer = jnp.where(over, layers - 1, me_layer - 1)
                    window = half - jnp.where(over, 1, 0)
                shift = lax.div(window + 2, 2) - 1
                target_half = window - 2 * shift
                source_row, target_row = (run, 0) if which == 0 else (1, run + 1)
                for side in range(2):
                    for piece, (first, count) in enumerate(pieces):
                        remote(windows[side].at[half, pl.ds(first, count), source_row],
                               windows[side].at[target_half, pl.ds(first, count), target_row],
                               far_edge_sem.at[side, target_half, which + piece],
                               me_group + shift, layer, act)

    def wait_far_edges(half, which):
        for side in range(2):
            for piece, (first, count) in enumerate((left_edge, right_edge)[which]):
                arrived(windows[side].at[half, pl.ds(first, count), 0 if which == 0 else run + 1],
                        far_edge_sem.at[side, half, which + piece])

    far_index = [
        list(range(band_first, band_first + band_count)) + list(range(rest, rest + 3))
        for rest in (rest_ahead, rest_behind)
    ]

    def right_tile(left, right, half, row):
        if left < WIDTH:
            return near[half, right, row + left]
        if left < WIDTH + 3:
            return ahead[half, far_index[0].index(right), row + left - WIDTH]
        return behind[half, far_index[1].index(right), row + left - WIDTH - 3]

    couples = [(0, 1), (2, 3), (4, 5), (6,), (7, 8), (9,), (10, 11), (12,)]

    def product(left_tile, half, row, finish):
        for couple in couples:
            tables = [dict(by_target[target]) for target in couple]
            lefts = sorted(set(left for table in tables for left in table))
            lhs = jnp.concatenate([left_tile(left) for left in lefts], axis=1)
            rhs = jnp.concatenate(
                [
                    jnp.concatenate(
                        [
                            right_tile(left, table[left], half, row)
                            if left in table
                            else jnp.zeros((size, size), jnp.bfloat16)
                            for table in tables
                        ],
                        axis=1,
                    )
                    for left in lefts
                ],
                axis=0,
            )
            total = jnp.dot(lhs, rhs, preferred_element_type=jnp.float32)
            for place, target in enumerate(couple):
                finish(target, total[:, place * size : (place + 1) * size])

    def row_at(position):
        inner = position < run - 2
        half = jnp.where(position < run, 1, 0)
        ends = jnp.where(position < run, (position - run + 2) * (run - 1), position - run)
        return half, jnp.where(inner, position + 1, ends)

    def computed_after(step):
        since = step - run
        early = jnp.where(since < 3, jnp.maximum(since, 0), jnp.minimum(2 * since - 2, run - 2))
        place = step - LAG - run
        late = jnp.where(place < 2, run - 1, run + place - 1)
        late = jnp.where(place >= run - 1, steps, late)
        return jnp.where(place < 1, early, late)

    def compute(position):
        half, row = row_at(position)
        for at_half, at_row, wait in (
            (1, 1, lambda: wait_near_edges(1, 0)),
            (1, run - BAND, lambda: wait_near_edges(1, 1)),
            (1, 0, lambda: wait_far_edges(1, 0)),
            (1, run - 1, lambda: wait_far_edges(1, 1)),
            (0, 0, lambda: (wait_near_edges(0, 0), wait_far_edges(0, 0))),
            (0, run - BAND, lambda: wait_near_edges(0, 1)),
            (0, run - 1, lambda: wait_far_edges(0, 1)),
        ):

            @pl.when(jnp.logical_and(half == at_half, row == at_row))
            def _():
                wait()

        global_row = half * period + me_layer * run + row

        def weight(target):
            return presence[target, global_row].astype(jnp.float32)

        def store_square(target, total):
            squared[target] = (total * weight(target)).astype(jnp.bfloat16)

        def store_result(target, total):
            third = total * weight(target)
            result = (3.0 * squared[target].astype(jnp.float32) - 2.0 * third).astype(jnp.bfloat16)
            for layer in range(layers):
                done[position, layer, target] = result[layer * part : (layer + 1) * part]

        product(lambda left: near[half, left, row + BAND], half, row, store_square)
        product(lambda left: squared[left], half, row, store_result)

    def each_result(position, act, act_local):
        half, row = row_at(position)
        target = out.at[:, half * period + me_layer * run + row]
        for turn in range(layers):
            layer = lax.rem(me_layer + turn, layers)
            source = done.at[position, layer]
            if turn == 0:
                if act_local is not None:
                    act_local(pltpu.make_async_copy(source, target, out_sem))
            else:
                remote(source, target, out_sem, me_group, layer, act, out_send_sem)

    @pl.loop(0, steps)
    def _(step):
        loads(step, start)

    for step in range(2):
        prepare(step)

    def near_until(step):
        return jnp.where(step < 0, 0, jnp.minimum(FIRST + RATE * step, steps))

    @pl.loop(0, steps + LAG)
    def _(step):
        other = step - run // 2

        @pl.when(jnp.logical_and(other >= 0, other < run))
        def _():
            wait_near(1, row_of(other))

        @pl.when(step < DIRECT)
        def _():
            far_sends(step, start)

        send_near(near_until(step - 1), near_until(step))

        @pl.when(jnp.logical_and(near_until(step - 1) < steps, near_until(step) == steps))
        def _():
            for side in range(2):
                near_edges(side, start, start)

        @pl.when(jnp.logical_and(step >= DIRECT, step < steps))
        def _():
            @pl.when(step < run)
            def _():
                wait_near(0, row_of(step))

            far_sends(step, start)

        @pl.when(step == run)
        def _():
            for early in range(DIRECT):
                wait_near(0, row_of(jnp.int32(early)))

        @pl.when(jnp.logical_and(step >= RELAY_LAG, step < steps + RELAY_LAG))
        def _():
            far_relays(step - RELAY_LAG, start, True)

        @pl.when(step >= LAG)
        def _():
            settled = step - LAG
            wait_far(settled)
            far_edges(settled, start)

            @pl.loop(computed_after(step - 1), computed_after(step))
            def _(position):
                compute(position)

                @pl.when(position > 0)
                def _():
                    each_result(position - 1, start, start)

    each_result(steps - 1, start, start)
    wait_near_sends()

    @pl.loop(0, steps)
    def _(step):
        far_sends(step, wait_send)
        far_relays(step, wait_send, False)
        far_edges(step, wait_send)
        each_result(step, wait_send, None)

    arrived(out, out_sem)


def relay_plan(groups, local_rows, layers, by_target):
    total_rows = groups * local_rows
    period = math.gcd(FAR, total_rows)
    if local_rows != 2 * period or period % layers or (FAR // period) % 2 == 0 or period // layers < 2 * BAND + 2:
        return None
    by_side = []
    for first in (WIDTH, WIDTH + 3):
        lefts = range(first, first + 3)
        by_side.append(set(b for pairs in by_target for a, b in pairs if a in lefts))
    band = sorted(b for b in by_side[0] if b < WIDTH)
    wanted = [set(band) | set(range(WIDTH + 3, WIDTH + 6)), set(band) | set(range(WIDTH, WIDTH + 3))]
    if by_side != wanted or band != list(range(band[0], band[0] + len(band))):
        return None
    return period, period // layers, (band[0], len(band), WIDTH + 3, WIDTH)


def relay_call(sizes, needed, by_target, blocks, presence):
    run, part, size = sizes[-3:]
    diagonals = blocks.shape[0]
    layers = sizes[2]
    far = needed[1] + 3
    return pl.pallas_call(
        functools.partial(relay_kernel, sizes, needed, by_target),
        out_shape=pltpu.VMEM(blocks.shape, jnp.bfloat16),
        in_specs=[pl.BlockSpec(memory_space=pl.ANY), pl.BlockSpec(memory_space=pltpu.SMEM)],
        out_specs=pl.BlockSpec(memory_space=pltpu.VMEM),
        scratch_shapes=[
            pltpu.VMEM(blocks.shape, jnp.bfloat16),
            pltpu.VMEM((2, diagonals, run + 2 * BAND, size, size), jnp.bfloat16),
            pltpu.VMEM((2, far, run + 2, size, size), jnp.bfloat16),
            pltpu.VMEM((2, far, run + 2, size, size), jnp.bfloat16),
            pltpu.VMEM((diagonals, size, size), jnp.bfloat16),
            pltpu.VMEM((2 * run, layers, diagonals, part, size), jnp.bfloat16),
            pltpu.SemaphoreType.DMA((2 * run, layers)),
            pltpu.SemaphoreType.DMA,
            pltpu.SemaphoreType.DMA((2, run)),
            pltpu.SemaphoreType.DMA((2, 2 * BAND, 3)),
            pltpu.SemaphoreType.DMA((2, 2, run)),
            pltpu.SemaphoreType.DMA((2, 2, run)),
            pltpu.SemaphoreType.DMA((2, 2, 3)),
            pltpu.SemaphoreType.DMA,
            pltpu.SemaphoreType.DMA,
        ],
        compiler_params=pltpu.CompilerParams(has_side_effects=True, vmem_limit_bytes=44 * 2**20),
    )(blocks, presence)


def solution(mesh):
    columns = mesh.shape["col"]
    layers = mesh.shape["layer"]
    groups = mesh.shape["row"] * columns

    def per_device(blocks, presence):
        diagonals, local_rows, part, size = blocks.shape
        total_rows = local_rows * groups
        rows = local_rows // layers
        offsets = offset_table(total_rows)
        by_target = pair_table(offsets, total_rows)
        plan = relay_plan(groups, local_rows, layers, by_target)
        if plan is not None:
            period, run, needed = plan
            sizes = (groups, columns, layers, local_rows, period, run, part, size)
            return relay_call(sizes, needed, by_target, blocks, presence)
        needed = []
        for first in (WIDTH, WIDTH + 3):
            lefts = range(first, first + 3)
            needed.append(sorted(set(b for pairs in by_target for a, b in pairs if a in lefts)))
        masked = blocks * presence.astype(jnp.bfloat16)[:, :, None, None]
        sizes = (groups, columns, layers, local_rows, rows, part, size)
        return pl.pallas_call(
            functools.partial(direct_kernel, sizes, needed, by_target),
            out_shape=jax.ShapeDtypeStruct(blocks.shape, jnp.bfloat16),
            in_specs=[pl.BlockSpec(memory_space=pl.ANY), pl.BlockSpec(memory_space=pltpu.SMEM)],
            out_specs=pl.BlockSpec(memory_space=pl.ANY),
            scratch_shapes=[
                pltpu.VMEM((layers, diagonals, rows + 2 * BAND, part, size), jnp.bfloat16),
                pltpu.VMEM((layers, len(needed[0]), rows + 2, part, size), jnp.bfloat16),
                pltpu.VMEM((layers, len(needed[1]), rows + 2, part, size), jnp.bfloat16),
                pltpu.VMEM((diagonals, size, size), jnp.bfloat16),
                pltpu.VMEM((rows, layers, diagonals, part, size), jnp.bfloat16),
                pltpu.SemaphoreType.DMA,
                pltpu.SemaphoreType.DMA((rows,)),
                pltpu.SemaphoreType.DMA((rows,)),
                pltpu.SemaphoreType.DMA((rows,)),
                pltpu.SemaphoreType.DMA,
                pltpu.SemaphoreType.DMA,
            ],
            compiler_params=pltpu.CompilerParams(has_side_effects=True, vmem_limit_bytes=48 * 2**20),
        )(masked, presence)

    return jax.shard_map(
        per_device,
        mesh=mesh,
        in_specs=(P(None, ("row", "col"), "layer", None), P(None, ("row", "col"))),
        out_specs=P(None, ("row", "col"), "layer", None),
        check_vma=False,
    )
```

```python
import functools
import math

import jax
import jax.numpy as jnp
from jax import lax
from jax.experimental import pallas as pl
from jax.experimental.pallas import tpu as pltpu
from jax.sharding import PartitionSpec as P

BAND = 3
FAR = 160
CHUNKS = 8
RELAY_LAG = 2
LAG = 3
DIRECT = 1
FIRST = 16
RATE = 1
WIDTH = 2 * BAND + 1
MESH = pl.DeviceIdType.MESH


def offset_table(total_rows):
    values = list(range(-BAND, BAND + 1))
    values = values + [FAR - 1, FAR, FAR + 1, -FAR - 1, -FAR, -FAR + 1]
    return [value % total_rows for value in values]


def pair_table(offsets, total_rows):
    by_target = []
    for target in offsets:
        entries = []
        for left_index, left in enumerate(offsets):
            for right_index, right in enumerate(offsets):
                if (left + right) % total_rows == target:
                    entries.append((left_index, right_index))
        by_target.append(entries)
    return by_target


def runs_of(indices):
    runs = []
    for position, index in enumerate(indices):
        if runs and runs[-1][1] + runs[-1][2] == index:
            runs[-1][2] += 1
        else:
            runs.append([position, index, 1])
    return runs


def pieces_of(low, high, local_rows):
    for ahead in range(low // local_rows, (high - 1) // local_rows + 1):
        first = max(low, ahead * local_rows)
        last = min(high, (ahead + 1) * local_rows)
        yield ahead, first - ahead * local_rows, last - first, first - low


def direct_kernel(sizes, needed, by_target, tiles, presence, out, near, ahead_far, behind_far, squared, done,
           send_sem, near_sem, ahead_sem, behind_sem, out_send_sem, out_sem):
    groups, columns, layers, local_rows, rows, part, size = sizes
    me_layer = lax.axis_index("layer")
    me_group = lax.axis_index("row") * columns + lax.axis_index("col")

    def device(steps, layer):
        group = lax.rem(me_group + steps % groups, groups)
        return {"row": lax.div(group, columns), "col": lax.rem(group, columns), "layer": layer}

    everything = list(range(len(by_target)))
    windows = [
        (near, near_sem, -BAND, 2 * BAND, everything),
        (ahead_far, ahead_sem, FAR - 1, 2, needed[0]),
        (behind_far, behind_sem, -FAR - 1, 2, needed[1]),
    ]
    chunks = CHUNKS if rows % CHUNKS == 0 else rows
    step_rows = rows // chunks

    def chunk_rows(chunk, extra):
        first = 0 if chunk == 0 else chunk * step_rows + extra
        return first, (chunk + 1) * step_rows + extra

    def copies_to(chunk, layer, act_remote, act_local):
        for window, sem, low, extra, diagonals in windows:
            first, last = chunk_rows(chunk, extra)
            start_row = low + layer * rows
            for steps, source_row, count, window_row in pieces_of(
                start_row + first, start_row + last, local_rows
            ):
                for position, index, length in runs_of(diagonals):
                    source = tiles.at[pl.ds(index, length), pl.ds(source_row, count)]
                    target = window.at[me_layer, pl.ds(position, length), pl.ds(first + window_row, count)]

                    def remote():
                        act_remote(
                            pltpu.make_async_remote_copy(
                                src_ref=source, dst_ref=target, send_sem=send_sem, recv_sem=sem.at[chunk],
                                device_id=device(-steps, layer), device_id_type=MESH,
                            )
                        )

                    def local():
                        if act_local is not None:
                            act_local(pltpu.make_async_copy(source, target, sem.at[chunk]))

                    if steps % groups == 0:
                        pl.when(me_layer != layer)(remote)
                        pl.when(me_layer == layer)(local)
                    else:
                        remote()

    def start(copy):
        copy.start()

    for chunk in range(chunks):
        for turn in range(layers):
            for layer in range(layers):

                @pl.when(lax.rem(me_layer + turn, layers) == layer)
                def _():
                    copies_to(chunk, layer, start, start)

    def wait_for(chunk):
        for window, sem, _, extra, _ in windows:
            first, last = chunk_rows(chunk, extra)
            arrived = window.at[:, :, pl.ds(first, last - first)]
            pltpu.make_async_copy(arrived, arrived, sem.at[chunk]).wait()

    def tile_of(window, index, row):
        return jnp.concatenate([window[layer, index, row] for layer in range(layers)], axis=0)

    def right_tile(left, right, row):
        if left < WIDTH:
            return tile_of(near, right, row + left)
        if left < WIDTH + 3:
            return tile_of(ahead_far, needed[0].index(right), row + left - WIDTH)
        return tile_of(behind_far, needed[1].index(right), row + left - WIDTH - 3)

    couples = [(0, 1), (2, 3), (4, 5), (6,), (7, 8), (9,), (10, 11), (12,)]

    def product(left_tile, row, finish):
        for couple in couples:
            tables = [dict(by_target[target]) for target in couple]
            lefts = sorted(set(left for table in tables for left in table))
            lhs = jnp.concatenate([left_tile(left) for left in lefts], axis=1)
            rhs = jnp.concatenate(
                [
                    jnp.concatenate(
                        [
                            right_tile(left, table[left], row)
                            if left in table
                            else jnp.zeros((size, size), jnp.bfloat16)
                            for table in tables
                        ],
                        axis=1,
                    )
                    for left in lefts
                ],
                axis=0,
            )
            total = jnp.dot(lhs, rhs, preferred_element_type=jnp.float32)
            for place, target in enumerate(couple):
                finish(target, total[:, place * size : (place + 1) * size])

    def each_result(row, act_remote, act_local):
        place = me_layer * rows + row
        for layer in range(layers):
            source = done.at[row, layer]
            target = out.at[:, place]

            def remote():
                act_remote(
                    pltpu.make_async_remote_copy(
                        src_ref=source, dst_ref=target, send_sem=out_send_sem, recv_sem=out_sem,
                        device_id=device(0, layer), device_id_type=MESH,
                    )
                )

            def local():
                if act_local is not None:
                    act_local(pltpu.make_async_copy(source, target, out_sem))

            pl.when(me_layer != layer)(remote)
            pl.when(me_layer == layer)(local)

    @pl.loop(0, rows)
    def _(row):
        for chunk in range(chunks):

            @pl.when(row == chunk * step_rows)
            def _():
                wait_for(chunk)

        def weight(target):
            return presence[target, me_layer * rows + row].astype(jnp.float32)

        def store_square(target, total):
            squared[target] = (total * weight(target)).astype(jnp.bfloat16)

        def store_result(target, total):
            third = total * weight(target)
            result = (3.0 * squared[target].astype(jnp.float32) - 2.0 * third).astype(jnp.bfloat16)
            for layer in range(layers):
                done[row, layer, target] = result[layer * part : (layer + 1) * part]

        product(lambda left: tile_of(near, left, row + BAND), row, store_square)
        product(lambda left: squared[left], row, store_result)

        @pl.when(row > 0)
        def _():
            each_result(row - 1, start, start)

    each_result(rows - 1, start, start)
    for chunk in range(chunks):
        for layer in range(layers):
            copies_to(chunk, layer, lambda copy: copy.wait_send(), None)

    @pl.loop(0, rows)
    def _(row):
        each_result(row, lambda copy: copy.wait_send(), None)

    pltpu.make_async_copy(out, out, out_sem).wait()


def relay_kernel(sizes, needed, by_target, blocks, presence, out, tiles, near, ahead, behind, squared, done,
                 load_sem, send_sem, near_sem, near_edge_sem, far_band_sem, far_rest_sem, far_edge_sem, out_send_sem, out_sem):
    groups, columns, layers, local_rows, period, run, part, size = sizes
    steps = 2 * run
    distance = FAR // period
    band_first, band_count, rest_ahead, rest_behind = needed
    far_count = band_count + 3
    me_layer = lax.axis_index("layer")
    me_group = lax.axis_index("row") * columns + lax.axis_index("col")
    me_column = lax.axis_index("col")
    windows = (ahead, behind)

    def start(copy):
        copy.start()

    def wait_send(copy):
        copy.wait_send()

    def remote(source, target, sem, group, layer, act, sent=send_sem):
        group = lax.rem(group + 2 * groups, groups)
        act(
            pltpu.make_async_remote_copy(
                src_ref=source, dst_ref=target, send_sem=sent, recv_sem=sem,
                device_id={"row": lax.div(group, columns), "col": lax.rem(group, columns), "layer": layer},
                device_id_type=MESH,
            )
        )

    def arrived(view, sem):
        pltpu.make_async_copy(view, view, sem).wait()

    mine = pl.ds(pl.multiple_of(me_layer * part, part), part)

    def near_copies(half, place, first, count, sem, act, act_local):
        for turn in range(layers):
            layer = lax.rem(me_layer + turn, layers)
            row = half * period + layer * run + place - BAND
            ahead_groups = lax.div(row + local_rows, local_rows) - 1
            source = tiles.at[pl.ds(first, count), row - ahead_groups * local_rows]
            target = near.at[half, pl.ds(first, count), place, mine]

            def send():
                remote(source, target, sem, me_group - ahead_groups, layer, act)

            def local():
                if act_local is not None:
                    act_local(pltpu.make_async_copy(source, target, sem))

            if turn == 0:
                pl.when(ahead_groups != 0)(send)
                pl.when(ahead_groups == 0)(local)
            else:
                send()

    def edge_pieces(side):
        for position in range(BAND):
            place = position if side == 0 else run + BAND + position
            used = set()
            for pairs in by_target:
                for left, right in pairs:
                    if left < WIDTH and 0 <= place - left < run:
                        used.add(right)
            for piece, (_, first, count) in enumerate(runs_of(sorted(used))):
                yield side * BAND + position, place, piece, first, count

    def near_edges(side, act, act_local):
        for edge, place, piece, first, count in edge_pieces(side):
            for half in range(2):
                near_copies(half, place, first, count, near_edge_sem.at[half, edge, piece], act, act_local)

    def wait_near_edges(half, side):
        for edge, place, piece, first, count in edge_pieces(side):
            arrived(near.at[half, pl.ds(first, count), place], near_edge_sem.at[half, edge, piece])

    def row_of(step):
        return lax.rem(step + run - 1, run)

    def near_step(step, act, act_local):
        half = lax.div(step, run)
        row = row_of(step)
        near_copies(half, row + BAND, 0, len(by_target), near_sem.at[half, row], act, act_local)

    def own_row(step, layer):
        return lax.div(step, run) * period + layer * run + row_of(step)

    def loads(step, act):
        for layer in range(layers):
            row = own_row(step, layer)
            act(pltpu.make_async_copy(blocks.at[:, row], tiles.at[:, row], load_sem.at[step, layer]))

    def mask(step):
        for layer in range(layers):
            row = own_row(step, layer)
            for target in range(len(by_target)):
                weight = presence[target, row].astype(jnp.float32)
                tiles[target, row] = (tiles[target, row].astype(jnp.float32) * weight).astype(jnp.bfloat16)

    def prepare(step):
        @pl.when(step < steps)
        def _():
            loads(step, lambda copy: copy.wait())
            mask(step)

    def send_near(first, last):
        @pl.loop(first, last)
        def _(step):
            prepare(step + 2)
            near_step(step, start, start)

    def wait_near_sends():
        @pl.loop(0, steps)
        def _(step):
            near_step(step, wait_send, None)

        for side in range(2):
            near_edges(side, wait_send, None)

    def wait_near(half, row):
        arrived(near.at[half, :, row + BAND], near_sem.at[half, row])

    def moves(phase):
        lower = (-distance // 2, (1 - distance) // 2)
        upper = (distance // 2, (1 + distance) // 2)
        return (
            jnp.where(phase == 0, lower[0], lower[1]),
            jnp.where(phase == 0, upper[0], upper[1]),
        )

    def relays(phase, column):
        down, up = moves(phase)
        column = lax.rem(column + 4 * groups, columns)
        first = lax.rem(column + down + 4 * groups, columns) - column
        second = lax.rem(column + up + 4 * groups, columns) - column
        alike = first * second > 0
        middle = columns // 2

        def crosses(shift):
            return (column < middle) != (column + shift < middle)

        nearer = jnp.abs(first) <= jnp.abs(second)
        return (
            alike & nearer & crosses(first),
            alike & jnp.logical_not(nearer) & crosses(second),
        )

    def far_sends(step, act):
        phase = lax.div(step, run)
        row = row_of(step)
        half = 1 - phase
        shifts = moves(phase)
        passes = relays(phase, me_column)

        def send(side, first, count, place, sem):
            group = me_group + shifts[side]

            @pl.when(step < DIRECT)
            def _():
                for turn in range(layers):
                    layer = lax.rem(me_layer + turn, layers)
                    remote(tiles.at[pl.ds(first, count), own_row(step, layer)],
                           windows[side].at[half, pl.ds(place, count), row + 1, mine],
                           sem, group, layer, act)

            @pl.when(step >= DIRECT)
            def _():
                remote(near.at[phase, pl.ds(first, count), row + BAND],
                       windows[side].at[half, pl.ds(place, count), row + 1],
                       sem, group, me_layer, act)

        def send_side(side):
            @pl.when(jnp.logical_not(passes[1 - side]))
            def _():
                send(side, band_first, band_count, 0, far_band_sem.at[side, half, row])

            send(side, (rest_ahead, rest_behind)[side], 3, band_count, far_rest_sem.at[side, half, row])

        cores = [lax.div(lax.rem(me_group + shift + 2 * groups, groups), columns) for shift in shifts]
        later = cores[0] < cores[1]
        pl.when(jnp.logical_not(later))(lambda: send_side(0))
        send_side(1)
        pl.when(later)(lambda: send_side(0))

    def passes_on(phase):
        shifts = moves(phase)
        return [relays(phase, me_column - shifts[side])[side] for side in range(2)]

    def far_relays(step, act, wait):
        phase = lax.div(step, run)
        row = row_of(step)
        half = 1 - phase
        shifts = moves(phase)
        for side, passing in enumerate(passes_on(phase)):

            @pl.when(passing)
            def _():
                view = windows[side].at[half, pl.ds(0, band_count), row + 1]
                if wait:
                    arrived(view, far_band_sem.at[side, half, row])
                remote(view, windows[1 - side].at[half, pl.ds(0, band_count), row + 1],
                       far_band_sem.at[1 - side, half, row],
                       me_group - shifts[side] + shifts[1 - side], me_layer, act)

    def wait_far(step):
        phase = lax.div(step, run)
        row = row_of(step)
        half = 1 - phase
        for side, passing in enumerate(passes_on(phase)):

            @pl.when(jnp.logical_not(passing))
            def _():
                arrived(windows[side].at[half, pl.ds(0, band_count), row + 1], far_band_sem.at[side, half, row])

            arrived(windows[side].at[half, pl.ds(band_count, 3), row + 1], far_rest_sem.at[side, half, row])

    middle = band_count // 2
    left_edge = [(middle, far_count - middle)]
    right_edge = [(0, middle + 1), (band_count, 3)]

    def far_edges(step, act):
        half = 1 - lax.div(step, run)
        place = lax.rem(step, run)
        for which, pieces in enumerate((left_edge, right_edge)):

            @pl.when(place == which)
            def _():
                if which == 0:
                    over = me_layer == layers - 1
                    layer = jnp.where(over, 0, me_layer + 1)
                    window = half + jnp.where(over, 1, 0)
                else:
                    over = me_layer == 0
                    layer = jnp.where(over, layers - 1, me_layer - 1)
                    window = half - jnp.where(over, 1, 0)
                shift = lax.div(window + 2, 2) - 1
                target_half = window - 2 * shift
                source_row, target_row = (run, 0) if which == 0 else (1, run + 1)
                for side in range(2):
                    for piece, (first, count) in enumerate(pieces):
                        remote(windows[side].at[half, pl.ds(first, count), source_row],
                               windows[side].at[target_half, pl.ds(first, count), target_row],
                               far_edge_sem.at[side, target_half, which + piece],
                               me_group + shift, layer, act)

    def wait_far_edges(half, which):
        for side in range(2):
            for piece, (first, count) in enumerate((left_edge, right_edge)[which]):
                arrived(windows[side].at[half, pl.ds(first, count), 0 if which == 0 else run + 1],
                        far_edge_sem.at[side, half, which + piece])

    far_index = [
        list(range(band_first, band_first + band_count)) + list(range(rest, rest + 3))
        for rest in (rest_ahead, rest_behind)
    ]

    def right_tile(left, right, half, row):
        if left < WIDTH:
            return near[half, right, row + left]
        if left < WIDTH + 3:
            return ahead[half, far_index[0].index(right), row + left - WIDTH]
        return behind[half, far_index[1].index(right), row + left - WIDTH - 3]

    couples = [(0, 1), (2, 3), (4, 5), (6,), (7, 8), (9,), (10, 11), (12,)]

    def product(left_tile, half, row, finish):
        for couple in couples:
            tables = [dict(by_target[target]) for target in couple]
            lefts = sorted(set(left for table in tables for left in table))
            lhs = jnp.concatenate([left_tile(left) for left in lefts], axis=1)
            rhs = jnp.concatenate(
                [
                    jnp.concatenate(
                        [
                            right_tile(left, table[left], half, row)
                            if left in table
                            else jnp.zeros((size, size), jnp.bfloat16)
                            for table in tables
                        ],
                        axis=1,
                    )
                    for left in lefts
                ],
                axis=0,
            )
            total = jnp.dot(lhs, rhs, preferred_element_type=jnp.float32)
            for place, target in enumerate(couple):
                finish(target, total[:, place * size : (place + 1) * size])

    def row_at(position):
        inner = position < run - 2
        half = jnp.where(position < run, 1, 0)
        ends = jnp.where(position < run, (position - run + 2) * (run - 1), position - run)
        return half, jnp.where(inner, position + 1, ends)

    def computed_after(step):
        since = step - run
        early = jnp.where(since < 3, jnp.maximum(since, 0), jnp.minimum(2 * since - 2, run - 2))
        place = step - LAG - run
        late = jnp.where(place < 2, run - 1, run + place - 1)
        late = jnp.where(place >= run - 1, steps, late)
        return jnp.where(place < 1, early, late)

    def compute(position):
        half, row = row_at(position)
        for at_half, at_row, wait in (
            (1, 1, lambda: wait_near_edges(1, 0)),
            (1, run - BAND, lambda: wait_near_edges(1, 1)),
            (1, 0, lambda: wait_far_edges(1, 0)),
            (1, run - 1, lambda: wait_far_edges(1, 1)),
            (0, 0, lambda: (wait_near_edges(0, 0), wait_far_edges(0, 0))),
            (0, run - BAND, lambda: wait_near_edges(0, 1)),
            (0, run - 1, lambda: wait_far_edges(0, 1)),
        ):

            @pl.when(jnp.logical_and(half == at_half, row == at_row))
            def _():
                wait()

        global_row = half * period + me_layer * run + row

        def weight(target):
            return presence[target, global_row].astype(jnp.float32)

        def store_square(target, total):
            squared[target] = (total * weight(target)).astype(jnp.bfloat16)

        def store_result(target, total):
            third = total * weight(target)
            result = (3.0 * squared[target].astype(jnp.float32) - 2.0 * third).astype(jnp.bfloat16)
            for layer in range(layers):
                done[position, layer, target] = result[layer * part : (layer + 1) * part]

        product(lambda left: near[half, left, row + BAND], half, row, store_square)
        product(lambda left: squared[left], half, row, store_result)

    def each_result(position, act, act_local):
        half, row = row_at(position)
        target = out.at[:, half * period + me_layer * run + row]
        for turn in range(layers):
            layer = lax.rem(me_layer + turn, layers)
            source = done.at[position, layer]
            if turn == 0:
                if act_local is not None:
                    act_local(pltpu.make_async_copy(source, target, out_sem))
            else:
                remote(source, target, out_sem, me_group, layer, act, out_send_sem)

    @pl.loop(0, steps)
    def _(step):
        loads(step, start)

    for step in range(2):
        prepare(step)

    def near_until(step):
        return jnp.where(step < 0, 0, jnp.minimum(FIRST + RATE * step, steps))

    @pl.loop(0, steps + LAG)
    def _(step):
        other = step - run // 2

        @pl.when(jnp.logical_and(other >= 0, other < run))
        def _():
            wait_near(1, row_of(other))

        @pl.when(step < DIRECT)
        def _():
            far_sends(step, start)

        send_near(near_until(step - 1), near_until(step))

        @pl.when(jnp.logical_and(near_until(step - 1) < steps, near_until(step) == steps))
        def _():
            for side in range(2):
                near_edges(side, start, start)

        @pl.when(jnp.logical_and(step >= DIRECT, step < steps))
        def _():
            @pl.when(step < run)
            def _():
                wait_near(0, row_of(step))

            far_sends(step, start)

        @pl.when(step == run)
        def _():
            for early in range(DIRECT):
                wait_near(0, row_of(jnp.int32(early)))

        @pl.when(jnp.logical_and(step >= RELAY_LAG, step < steps + RELAY_LAG))
        def _():
            far_relays(step - RELAY_LAG, start, True)

        @pl.when(step >= LAG)
        def _():
            settled = step - LAG
            wait_far(settled)
            far_edges(settled, start)

            @pl.loop(computed_after(step - 1), computed_after(step))
            def _(position):
                compute(position)

                @pl.when(position > 0)
                def _():
                    each_result(position - 1, start, start)

    each_result(steps - 1, start, start)
    wait_near_sends()

    @pl.loop(0, steps)
    def _(step):
        far_sends(step, wait_send)
        far_relays(step, wait_send, False)
        far_edges(step, wait_send)
        each_result(step, wait_send, None)

    arrived(out, out_sem)


def relay_plan(groups, local_rows, layers, by_target):
    total_rows = groups * local_rows
    period = math.gcd(FAR, total_rows)
    if local_rows != 2 * period or period % layers or (FAR // period) % 2 == 0 or period // layers < 2 * BAND + 2:
        return None
    by_side = []
    for first in (WIDTH, WIDTH + 3):
        lefts = range(first, first + 3)
        by_side.append(set(b for pairs in by_target for a, b in pairs if a in lefts))
    band = sorted(b for b in by_side[0] if b < WIDTH)
    wanted = [set(band) | set(range(WIDTH + 3, WIDTH + 6)), set(band) | set(range(WIDTH, WIDTH + 3))]
    if by_side != wanted or band != list(range(band[0], band[0] + len(band))):
        return None
    return period, period // layers, (band[0], len(band), WIDTH + 3, WIDTH)


def relay_call(sizes, needed, by_target, blocks, presence):
    run, part, size = sizes[-3:]
    diagonals = blocks.shape[0]
    layers = sizes[2]
    far = needed[1] + 3
    return pl.pallas_call(
        functools.partial(relay_kernel, sizes, needed, by_target),
        out_shape=pltpu.VMEM(blocks.shape, jnp.bfloat16),
        in_specs=[pl.BlockSpec(memory_space=pl.ANY), pl.BlockSpec(memory_space=pltpu.SMEM)],
        out_specs=pl.BlockSpec(memory_space=pltpu.VMEM),
        scratch_shapes=[
            pltpu.VMEM(blocks.shape, jnp.bfloat16),
            pltpu.VMEM((2, diagonals, run + 2 * BAND, size, size), jnp.bfloat16),
            pltpu.VMEM((2, far, run + 2, size, size), jnp.bfloat16),
            pltpu.VMEM((2, far, run + 2, size, size), jnp.bfloat16),
            pltpu.VMEM((diagonals, size, size), jnp.bfloat16),
            pltpu.VMEM((2 * run, layers, diagonals, part, size), jnp.bfloat16),
            pltpu.SemaphoreType.DMA((2 * run, layers)),
            pltpu.SemaphoreType.DMA,
            pltpu.SemaphoreType.DMA((2, run)),
            pltpu.SemaphoreType.DMA((2, 2 * BAND, 3)),
            pltpu.SemaphoreType.DMA((2, 2, run)),
            pltpu.SemaphoreType.DMA((2, 2, run)),
            pltpu.SemaphoreType.DMA((2, 2, 3)),
            pltpu.SemaphoreType.DMA,
            pltpu.SemaphoreType.DMA,
        ],
        compiler_params=pltpu.CompilerParams(has_side_effects=True, vmem_limit_bytes=44 * 2**20),
    )(blocks, presence)


def solution(mesh):
    columns = mesh.shape["col"]
    layers = mesh.shape["layer"]
    groups = mesh.shape["row"] * columns

    def per_device(blocks, presence):
        diagonals, local_rows, part, size = blocks.shape
        total_rows = local_rows * groups
        rows = local_rows // layers
        offsets = offset_table(total_rows)
        by_target = pair_table(offsets, total_rows)
        plan = relay_plan(groups, local_rows, layers, by_target)
        if plan is not None:
            period, run, needed = plan
            sizes = (groups, columns, layers, local_rows, period, run, part, size)
            return relay_call(sizes, needed, by_target, blocks, presence)
        needed = []
        for first in (WIDTH, WIDTH + 3):
            lefts = range(first, first + 3)
            needed.append(sorted(set(b for pairs in by_target for a, b in pairs if a in lefts)))
        masked = blocks * presence.astype(jnp.bfloat16)[:, :, None, None]
        sizes = (groups, columns, layers, local_rows, rows, part, size)
        return pl.pallas_call(
            functools.partial(direct_kernel, sizes, needed, by_target),
            out_shape=jax.ShapeDtypeStruct(blocks.shape, jnp.bfloat16),
            in_specs=[pl.BlockSpec(memory_space=pl.ANY), pl.BlockSpec(memory_space=pltpu.SMEM)],
            out_specs=pl.BlockSpec(memory_space=pl.ANY),
            scratch_shapes=[
                pltpu.VMEM((layers, diagonals, rows + 2 * BAND, part, size), jnp.bfloat16),
                pltpu.VMEM((layers, len(needed[0]), rows + 2, part, size), jnp.bfloat16),
                pltpu.VMEM((layers, len(needed[1]), rows + 2, part, size), jnp.bfloat16),
                pltpu.VMEM((diagonals, size, size), jnp.bfloat16),
                pltpu.VMEM((rows, layers, diagonals, part, size), jnp.bfloat16),
                pltpu.SemaphoreType.DMA,
                pltpu.SemaphoreType.DMA((rows,)),
                pltpu.SemaphoreType.DMA((rows,)),
                pltpu.SemaphoreType.DMA((rows,)),
                pltpu.SemaphoreType.DMA,
                pltpu.SemaphoreType.DMA,
            ],
            compiler_params=pltpu.CompilerParams(has_side_effects=True, vmem_limit_bytes=48 * 2**20),
        )(masked, presence)

    return jax.shard_map(
        per_device,
        mesh=mesh,
        in_specs=(P(None, ("row", "col"), "layer", None), P(None, ("row", "col"))),
        out_specs=P(None, ("row", "col"), "layer", None),
        check_vma=False,
    )
```

```python
import functools
import math

import jax
import jax.numpy as jnp
from jax import lax
from jax.experimental import pallas as pl
from jax.experimental.pallas import tpu as pltpu
from jax.sharding import PartitionSpec as P

BAND = 3
FAR = 160
CHUNKS = 8
RELAY_LAG = 2
LAG = 3
DIRECT = 1
FIRST = 16
RATE = 1
WIDTH = 2 * BAND + 1
MESH = pl.DeviceIdType.MESH


def offset_table(total_rows):
    values = list(range(-BAND, BAND + 1))
    values = values + [FAR - 1, FAR, FAR + 1, -FAR - 1, -FAR, -FAR + 1]
    return [value % total_rows for value in values]


def pair_table(offsets, total_rows):
    by_target = []
    for target in offsets:
        entries = []
        for left_index, left in enumerate(offsets):
            for right_index, right in enumerate(offsets):
                if (left + right) % total_rows == target:
                    entries.append((left_index, right_index))
        by_target.append(entries)
    return by_target


def runs_of(indices):
    runs = []
    for position, index in enumerate(indices):
        if runs and runs[-1][1] + runs[-1][2] == index:
            runs[-1][2] += 1
        else:
            runs.append([position, index, 1])
    return runs


def pieces_of(low, high, local_rows):
    for ahead in range(low // local_rows, (high - 1) // local_rows + 1):
        first = max(low, ahead * local_rows)
        last = min(high, (ahead + 1) * local_rows)
        yield ahead, first - ahead * local_rows, last - first, first - low


def direct_kernel(sizes, needed, by_target, tiles, presence, out, near, ahead_far, behind_far, squared, done,
           send_sem, near_sem, ahead_sem, behind_sem, out_send_sem, out_sem):
    groups, columns, layers, local_rows, rows, part, size = sizes
    me_layer = lax.axis_index("layer")
    me_group = lax.axis_index("row") * columns + lax.axis_index("col")

    def device(steps, layer):
        group = lax.rem(me_group + steps % groups, groups)
        return {"row": lax.div(group, columns), "col": lax.rem(group, columns), "layer": layer}

    everything = list(range(len(by_target)))
    windows = [
        (near, near_sem, -BAND, 2 * BAND, everything),
        (ahead_far, ahead_sem, FAR - 1, 2, needed[0]),
        (behind_far, behind_sem, -FAR - 1, 2, needed[1]),
    ]
    chunks = CHUNKS if rows % CHUNKS == 0 else rows
    step_rows = rows // chunks

    def chunk_rows(chunk, extra):
        first = 0 if chunk == 0 else chunk * step_rows + extra
        return first, (chunk + 1) * step_rows + extra

    def copies_to(chunk, layer, act_remote, act_local):
        for window, sem, low, extra, diagonals in windows:
            first, last = chunk_rows(chunk, extra)
            start_row = low + layer * rows
            for steps, source_row, count, window_row in pieces_of(
                start_row + first, start_row + last, local_rows
            ):
                for position, index, length in runs_of(diagonals):
                    source = tiles.at[pl.ds(index, length), pl.ds(source_row, count)]
                    target = window.at[me_layer, pl.ds(position, length), pl.ds(first + window_row, count)]

                    def remote():
                        act_remote(
                            pltpu.make_async_remote_copy(
                                src_ref=source, dst_ref=target, send_sem=send_sem, recv_sem=sem.at[chunk],
                                device_id=device(-steps, layer), device_id_type=MESH,
                            )
                        )

                    def local():
                        if act_local is not None:
                            act_local(pltpu.make_async_copy(source, target, sem.at[chunk]))

                    if steps % groups == 0:
                        pl.when(me_layer != layer)(remote)
                        pl.when(me_layer == layer)(local)
                    else:
                        remote()

    def start(copy):
        copy.start()

    for chunk in range(chunks):
        for turn in range(layers):
            for layer in range(layers):

                @pl.when(lax.rem(me_layer + turn, layers) == layer)
                def _():
                    copies_to(chunk, layer, start, start)

    def wait_for(chunk):
        for window, sem, _, extra, _ in windows:
            first, last = chunk_rows(chunk, extra)
            arrived = window.at[:, :, pl.ds(first, last - first)]
            pltpu.make_async_copy(arrived, arrived, sem.at[chunk]).wait()

    def tile_of(window, index, row):
        return jnp.concatenate([window[layer, index, row] for layer in range(layers)], axis=0)

    def right_tile(left, right, row):
        if left < WIDTH:
            return tile_of(near, right, row + left)
        if left < WIDTH + 3:
            return tile_of(ahead_far, needed[0].index(right), row + left - WIDTH)
        return tile_of(behind_far, needed[1].index(right), row + left - WIDTH - 3)

    couples = [(0, 1), (2, 3), (4, 5), (6,), (7, 8), (9,), (10, 11), (12,)]

    def product(left_tile, row, finish):
        for couple in couples:
            tables = [dict(by_target[target]) for target in couple]
            lefts = sorted(set(left for table in tables for left in table))
            lhs = jnp.concatenate([left_tile(left) for left in lefts], axis=1)
            rhs = jnp.concatenate(
                [
                    jnp.concatenate(
                        [
                            right_tile(left, table[left], row)
                            if left in table
                            else jnp.zeros((size, size), jnp.bfloat16)
                            for table in tables
                        ],
                        axis=1,
                    )
                    for left in lefts
                ],
                axis=0,
            )
            total = jnp.dot(lhs, rhs, preferred_element_type=jnp.float32)
            for place, target in enumerate(couple):
                finish(target, total[:, place * size : (place + 1) * size])

    def each_result(row, act_remote, act_local):
        place = me_layer * rows + row
        for layer in range(layers):
            source = done.at[row, layer]
            target = out.at[:, place]

            def remote():
                act_remote(
                    pltpu.make_async_remote_copy(
                        src_ref=source, dst_ref=target, send_sem=out_send_sem, recv_sem=out_sem,
                        device_id=device(0, layer), device_id_type=MESH,
                    )
                )

            def local():
                if act_local is not None:
                    act_local(pltpu.make_async_copy(source, target, out_sem))

            pl.when(me_layer != layer)(remote)
            pl.when(me_layer == layer)(local)

    @pl.loop(0, rows)
    def _(row):
        for chunk in range(chunks):

            @pl.when(row == chunk * step_rows)
            def _():
                wait_for(chunk)

        def weight(target):
            return presence[target, me_layer * rows + row].astype(jnp.float32)

        def store_square(target, total):
            squared[target] = (total * weight(target)).astype(jnp.bfloat16)

        def store_result(target, total):
            third = total * weight(target)
            result = (3.0 * squared[target].astype(jnp.float32) - 2.0 * third).astype(jnp.bfloat16)
            for layer in range(layers):
                done[row, layer, target] = result[layer * part : (layer + 1) * part]

        product(lambda left: tile_of(near, left, row + BAND), row, store_square)
        product(lambda left: squared[left], row, store_result)

        @pl.when(row > 0)
        def _():
            each_result(row - 1, start, start)

    each_result(rows - 1, start, start)
    for chunk in range(chunks):
        for layer in range(layers):
            copies_to(chunk, layer, lambda copy: copy.wait_send(), None)

    @pl.loop(0, rows)
    def _(row):
        each_result(row, lambda copy: copy.wait_send(), None)

    pltpu.make_async_copy(out, out, out_sem).wait()


def relay_kernel(sizes, needed, by_target, blocks, presence, out, tiles, near, ahead, behind, squared, done,
                 load_sem, send_sem, near_sem, near_edge_sem, far_band_sem, far_rest_sem, far_edge_sem, out_send_sem, out_sem):
    groups, columns, layers, local_rows, period, run, part, size = sizes
    steps = 2 * run
    distance = FAR // period
    band_first, band_count, rest_ahead, rest_behind = needed
    far_count = band_count + 3
    me_layer = lax.axis_index("layer")
    me_group = lax.axis_index("row") * columns + lax.axis_index("col")
    me_column = lax.axis_index("col")
    windows = (ahead, behind)

    def start(copy):
        copy.start()

    def wait_send(copy):
        copy.wait_send()

    def remote(source, target, sem, group, layer, act, sent=send_sem):
        group = lax.rem(group + 2 * groups, groups)
        act(
            pltpu.make_async_remote_copy(
                src_ref=source, dst_ref=target, send_sem=sent, recv_sem=sem,
                device_id={"row": lax.div(group, columns), "col": lax.rem(group, columns), "layer": layer},
                device_id_type=MESH,
            )
        )

    def arrived(view, sem):
        pltpu.make_async_copy(view, view, sem).wait()

    mine = pl.ds(pl.multiple_of(me_layer * part, part), part)

    def near_copies(half, place, first, count, sem, act, act_local):
        for turn in range(layers):
            layer = lax.rem(me_layer + turn, layers)
            row = half * period + layer * run + place - BAND
            ahead_groups = lax.div(row + local_rows, local_rows) - 1
            source = tiles.at[pl.ds(first, count), row - ahead_groups * local_rows]
            target = near.at[half, pl.ds(first, count), place, mine]

            def send():
                remote(source, target, sem, me_group - ahead_groups, layer, act)

            def local():
                if act_local is not None:
                    act_local(pltpu.make_async_copy(source, target, sem))

            if turn == 0:
                pl.when(ahead_groups != 0)(send)
                pl.when(ahead_groups == 0)(local)
            else:
                send()

    def edge_pieces(side):
        for position in range(BAND):
            place = position if side == 0 else run + BAND + position
            used = set()
            for pairs in by_target:
                for left, right in pairs:
                    if left < WIDTH and 0 <= place - left < run:
                        used.add(right)
            for piece, (_, first, count) in enumerate(runs_of(sorted(used))):
                yield side * BAND + position, place, piece, first, count

    def near_edges(side, act, act_local):
        for edge, place, piece, first, count in edge_pieces(side):
            for half in range(2):
                near_copies(half, place, first, count, near_edge_sem.at[half, edge, piece], act, act_local)

    def wait_near_edges(half, side):
        for edge, place, piece, first, count in edge_pieces(side):
            arrived(near.at[half, pl.ds(first, count), place], near_edge_sem.at[half, edge, piece])

    def row_of(step):
        return lax.rem(step + run - 1, run)

    def near_step(step, act, act_local):
        half = lax.div(step, run)
        row = row_of(step)
        near_copies(half, row + BAND, 0, len(by_target), near_sem.at[half, row], act, act_local)

    def own_row(step, layer):
        return lax.div(step, run) * period + layer * run + row_of(step)

    def loads(step, act):
        for layer in range(layers):
            row = own_row(step, layer)
            act(pltpu.make_async_copy(blocks.at[:, row], tiles.at[:, row], load_sem.at[step, layer]))

    def mask(step):
        for layer in range(layers):
            row = own_row(step, layer)
            for target in range(len(by_target)):
                weight = presence[target, row].astype(jnp.float32)
                tiles[target, row] = (tiles[target, row].astype(jnp.float32) * weight).astype(jnp.bfloat16)

    def prepare(step):
        @pl.when(step < steps)
        def _():
            loads(step, lambda copy: copy.wait())
            mask(step)

    def send_near(first, last):
        @pl.loop(first, last)
        def _(step):
            prepare(step + 2)
            near_step(step, start, start)

    def wait_near_sends():
        @pl.loop(0, steps)
        def _(step):
            near_step(step, wait_send, None)

        for side in range(2):
            near_edges(side, wait_send, None)

    def wait_near(half, row):
        arrived(near.at[half, :, row + BAND], near_sem.at[half, row])

    def moves(phase):
        lower = (-distance // 2, (1 - distance) // 2)
        upper = (distance // 2, (1 + distance) // 2)
        return (
            jnp.where(phase == 0, lower[0], lower[1]),
            jnp.where(phase == 0, upper[0], upper[1]),
        )

    def relays(phase, column):
        down, up = moves(phase)
        column = lax.rem(column + 4 * groups, columns)
        first = lax.rem(column + down + 4 * groups, columns) - column
        second = lax.rem(column + up + 4 * groups, columns) - column
        alike = first * second > 0
        middle = columns // 2

        def crosses(shift):
            return (column < middle) != (column + shift < middle)

        nearer = jnp.abs(first) <= jnp.abs(second)
        return (
            alike & nearer & crosses(first),
            alike & jnp.logical_not(nearer) & crosses(second),
        )

    def far_sends(step, act):
        phase = lax.div(step, run)
        row = row_of(step)
        half = 1 - phase
        shifts = moves(phase)
        passes = relays(phase, me_column)

        def send(side, first, count, place, sem):
            group = me_group + shifts[side]

            @pl.when(step < DIRECT)
            def _():
                for turn in range(layers):
                    layer = lax.rem(me_layer + turn, layers)
                    remote(tiles.at[pl.ds(first, count), own_row(step, layer)],
                           windows[side].at[half, pl.ds(place, count), row + 1, mine],
                           sem, group, layer, act)

            @pl.when(step >= DIRECT)
            def _():
                remote(near.at[phase, pl.ds(first, count), row + BAND],
                       windows[side].at[half, pl.ds(place, count), row + 1],
                       sem, group, me_layer, act)

        def send_side(side):
            @pl.when(jnp.logical_not(passes[1 - side]))
            def _():
                send(side, band_first, band_count, 0, far_band_sem.at[side, half, row])

            send(side, (rest_ahead, rest_behind)[side], 3, band_count, far_rest_sem.at[side, half, row])

        cores = [lax.div(lax.rem(me_group + shift + 2 * groups, groups), columns) for shift in shifts]
        later = cores[0] < cores[1]
        pl.when(jnp.logical_not(later))(lambda: send_side(0))
        send_side(1)
        pl.when(later)(lambda: send_side(0))

    def passes_on(phase):
        shifts = moves(phase)
        return [relays(phase, me_column - shifts[side])[side] for side in range(2)]

    def far_relays(step, act, wait):
        phase = lax.div(step, run)
        row = row_of(step)
        half = 1 - phase
        shifts = moves(phase)
        for side, passing in enumerate(passes_on(phase)):

            @pl.when(passing)
            def _():
                view = windows[side].at[half, pl.ds(0, band_count), row + 1]
                if wait:
                    arrived(view, far_band_sem.at[side, half, row])
                remote(view, windows[1 - side].at[half, pl.ds(0, band_count), row + 1],
                       far_band_sem.at[1 - side, half, row],
                       me_group - shifts[side] + shifts[1 - side], me_layer, act)

    def wait_far(step):
        phase = lax.div(step, run)
        row = row_of(step)
        half = 1 - phase
        for side, passing in enumerate(passes_on(phase)):

            @pl.when(jnp.logical_not(passing))
            def _():
                arrived(windows[side].at[half, pl.ds(0, band_count), row + 1], far_band_sem.at[side, half, row])

            arrived(windows[side].at[half, pl.ds(band_count, 3), row + 1], far_rest_sem.at[side, half, row])

    middle = band_count // 2
    left_edge = [(middle, far_count - middle)]
    right_edge = [(0, middle + 1), (band_count, 3)]

    def far_edges(step, act):
        half = 1 - lax.div(step, run)
        place = lax.rem(step, run)
        for which, pieces in enumerate((left_edge, right_edge)):

            @pl.when(place == which)
            def _():
                if which == 0:
                    over = me_layer == layers - 1
                    layer = jnp.where(over, 0, me_layer + 1)
                    window = half + jnp.where(over, 1, 0)
                else:
                    over = me_layer == 0
                    layer = jnp.where(over, layers - 1, me_layer - 1)
                    window = half - jnp.where(over, 1, 0)
                shift = lax.div(window + 2, 2) - 1
                target_half = window - 2 * shift
                source_row, target_row = (run, 0) if which == 0 else (1, run + 1)
                for side in range(2):
                    for piece, (first, count) in enumerate(pieces):
                        remote(windows[side].at[half, pl.ds(first, count), source_row],
                               windows[side].at[target_half, pl.ds(first, count), target_row],
                               far_edge_sem.at[side, target_half, which + piece],
                               me_group + shift, layer, act)

    def wait_far_edges(half, which):
        for side in range(2):
            for piece, (first, count) in enumerate((left_edge, right_edge)[which]):
                arrived(windows[side].at[half, pl.ds(first, count), 0 if which == 0 else run + 1],
                        far_edge_sem.at[side, half, which + piece])

    far_index = [
        list(range(band_first, band_first + band_count)) + list(range(rest, rest + 3))
        for rest in (rest_ahead, rest_behind)
    ]

    def right_tile(left, right, half, row):
        if left < WIDTH:
            return near[half, right, row + left]
        if left < WIDTH + 3:
            return ahead[half, far_index[0].index(right), row + left - WIDTH]
        return behind[half, far_index[1].index(right), row + left - WIDTH - 3]

    couples = [(0, 1), (2, 3), (4, 5), (6,), (7, 8), (9,), (10, 11), (12,)]

    def product(left_tile, half, row, finish):
        for couple in couples:
            tables = [dict(by_target[target]) for target in couple]
            lefts = sorted(set(left for table in tables for left in table))
            lhs = jnp.concatenate([left_tile(left) for left in lefts], axis=1)
            rhs = jnp.concatenate(
                [
                    jnp.concatenate(
                        [
                            right_tile(left, table[left], half, row)
                            if left in table
                            else jnp.zeros((size, size), jnp.bfloat16)
                            for table in tables
                        ],
                        axis=1,
                    )
                    for left in lefts
                ],
                axis=0,
            )
            total = jnp.dot(lhs, rhs, preferred_element_type=jnp.float32)
            for place, target in enumerate(couple):
                finish(target, total[:, place * size : (place + 1) * size])

    def row_at(position):
        inner = position < run - 2
        half = jnp.where(position < run, 1, 0)
        ends = jnp.where(position < run, (position - run + 2) * (run - 1), position - run)
        return half, jnp.where(inner, position + 1, ends)

    def computed_after(step):
        since = step - run
        early = jnp.where(since < 3, jnp.maximum(since, 0), jnp.minimum(2 * since - 2, run - 2))
        place = step - LAG - run
        late = jnp.where(place < 2, run - 1, run + place - 1)
        late = jnp.where(place >= run - 1, steps, late)
        return jnp.where(place < 1, early, late)

    def compute(position):
        half, row = row_at(position)
        for at_half, at_row, wait in (
            (1, 1, lambda: wait_near_edges(1, 0)),
            (1, run - BAND, lambda: wait_near_edges(1, 1)),
            (1, 0, lambda: wait_far_edges(1, 0)),
            (1, run - 1, lambda: wait_far_edges(1, 1)),
            (0, 0, lambda: (wait_near_edges(0, 0), wait_far_edges(0, 0))),
            (0, run - BAND, lambda: wait_near_edges(0, 1)),
            (0, run - 1, lambda: wait_far_edges(0, 1)),
        ):

            @pl.when(jnp.logical_and(half == at_half, row == at_row))
            def _():
                wait()

        global_row = half * period + me_layer * run + row

        def weight(target):
            return presence[target, global_row].astype(jnp.float32)

        def store_square(target, total):
            squared[target] = (total * weight(target)).astype(jnp.bfloat16)

        def store_result(target, total):
            third = total * weight(target)
            result = (3.0 * squared[target].astype(jnp.float32) - 2.0 * third).astype(jnp.bfloat16)
            for layer in range(layers):
                done[position, layer, target] = result[layer * part : (layer + 1) * part]

        product(lambda left: near[half, left, row + BAND], half, row, store_square)
        product(lambda left: squared[left], half, row, store_result)

    def each_result(position, act, act_local):
        half, row = row_at(position)
        target = out.at[:, half * period + me_layer * run + row]
        for turn in range(layers):
            layer = lax.rem(me_layer + turn, layers)
            source = done.at[position, layer]
            if turn == 0:
                if act_local is not None:
                    act_local(pltpu.make_async_copy(source, target, out_sem))
            else:
                remote(source, target, out_sem, me_group, layer, act, out_send_sem)

    @pl.loop(0, steps)
    def _(step):
        loads(step, start)

    for step in range(2):
        prepare(step)

    def near_until(step):
        return jnp.where(step < 0, 0, jnp.minimum(FIRST + RATE * step, steps))

    @pl.loop(0, steps + LAG)
    def _(step):
        other = step - run // 2

        @pl.when(jnp.logical_and(other >= 0, other < run))
        def _():
            wait_near(1, row_of(other))

        @pl.when(step < DIRECT)
        def _():
            far_sends(step, start)

        send_near(near_until(step - 1), near_until(step))

        @pl.when(step == 1)
        def _():
            for side in range(2):
                near_edges(side, start, start)

        @pl.when(jnp.logical_and(step >= DIRECT, step < steps))
        def _():
            @pl.when(step < run)
            def _():
                wait_near(0, row_of(step))

            far_sends(step, start)

        @pl.when(step == run)
        def _():
            for early in range(DIRECT):
                wait_near(0, row_of(jnp.int32(early)))

        @pl.when(jnp.logical_and(step >= RELAY_LAG, step < steps + RELAY_LAG))
        def _():
            far_relays(step - RELAY_LAG, start, True)

        @pl.when(step >= LAG)
        def _():
            settled = step - LAG
            wait_far(settled)
            far_edges(settled, start)

            @pl.loop(computed_after(step - 1), computed_after(step))
            def _(position):
                compute(position)

                @pl.when(position > 0)
                def _():
                    each_result(position - 1, start, start)

    each_result(steps - 1, start, start)
    wait_near_sends()

    @pl.loop(0, steps)
    def _(step):
        far_sends(step, wait_send)
        far_relays(step, wait_send, False)
        far_edges(step, wait_send)
        each_result(step, wait_send, None)

    arrived(out, out_sem)


def relay_plan(groups, local_rows, layers, by_target):
    total_rows = groups * local_rows
    period = math.gcd(FAR, total_rows)
    if local_rows != 2 * period or period % layers or (FAR // period) % 2 == 0 or period // layers < 2 * BAND + 2:
        return None
    by_side = []
    for first in (WIDTH, WIDTH + 3):
        lefts = range(first, first + 3)
        by_side.append(set(b for pairs in by_target for a, b in pairs if a in lefts))
    band = sorted(b for b in by_side[0] if b < WIDTH)
    wanted = [set(band) | set(range(WIDTH + 3, WIDTH + 6)), set(band) | set(range(WIDTH, WIDTH + 3))]
    if by_side != wanted or band != list(range(band[0], band[0] + len(band))):
        return None
    return period, period // layers, (band[0], len(band), WIDTH + 3, WIDTH)


def relay_call(sizes, needed, by_target, blocks, presence):
    run, part, size = sizes[-3:]
    diagonals = blocks.shape[0]
    layers = sizes[2]
    far = needed[1] + 3
    return pl.pallas_call(
        functools.partial(relay_kernel, sizes, needed, by_target),
        out_shape=pltpu.VMEM(blocks.shape, jnp.bfloat16),
        in_specs=[pl.BlockSpec(memory_space=pl.ANY), pl.BlockSpec(memory_space=pltpu.SMEM)],
        out_specs=pl.BlockSpec(memory_space=pltpu.VMEM),
        scratch_shapes=[
            pltpu.VMEM(blocks.shape, jnp.bfloat16),
            pltpu.VMEM((2, diagonals, run + 2 * BAND, size, size), jnp.bfloat16),
            pltpu.VMEM((2, far, run + 2, size, size), jnp.bfloat16),
            pltpu.VMEM((2, far, run + 2, size, size), jnp.bfloat16),
            pltpu.VMEM((diagonals, size, size), jnp.bfloat16),
            pltpu.VMEM((2 * run, layers, diagonals, part, size), jnp.bfloat16),
            pltpu.SemaphoreType.DMA((2 * run, layers)),
            pltpu.SemaphoreType.DMA,
            pltpu.SemaphoreType.DMA((2, run)),
            pltpu.SemaphoreType.DMA((2, 2 * BAND, 3)),
            pltpu.SemaphoreType.DMA((2, 2, run)),
            pltpu.SemaphoreType.DMA((2, 2, run)),
            pltpu.SemaphoreType.DMA((2, 2, 3)),
            pltpu.SemaphoreType.DMA,
            pltpu.SemaphoreType.DMA,
        ],
        compiler_params=pltpu.CompilerParams(has_side_effects=True, vmem_limit_bytes=44 * 2**20),
    )(blocks, presence)


def solution(mesh):
    columns = mesh.shape["col"]
    layers = mesh.shape["layer"]
    groups = mesh.shape["row"] * columns

    def per_device(blocks, presence):
        diagonals, local_rows, part, size = blocks.shape
        total_rows = local_rows * groups
        rows = local_rows // layers
        offsets = offset_table(total_rows)
        by_target = pair_table(offsets, total_rows)
        plan = relay_plan(groups, local_rows, layers, by_target)
        if plan is not None:
            period, run, needed = plan
            sizes = (groups, columns, layers, local_rows, period, run, part, size)
            return relay_call(sizes, needed, by_target, blocks, presence)
        needed = []
        for first in (WIDTH, WIDTH + 3):
            lefts = range(first, first + 3)
            needed.append(sorted(set(b for pairs in by_target for a, b in pairs if a in lefts)))
        masked = blocks * presence.astype(jnp.bfloat16)[:, :, None, None]
        sizes = (groups, columns, layers, local_rows, rows, part, size)
        return pl.pallas_call(
            functools.partial(direct_kernel, sizes, needed, by_target),
            out_shape=jax.ShapeDtypeStruct(blocks.shape, jnp.bfloat16),
            in_specs=[pl.BlockSpec(memory_space=pl.ANY), pl.BlockSpec(memory_space=pltpu.SMEM)],
            out_specs=pl.BlockSpec(memory_space=pl.ANY),
            scratch_shapes=[
                pltpu.VMEM((layers, diagonals, rows + 2 * BAND, part, size), jnp.bfloat16),
                pltpu.VMEM((layers, len(needed[0]), rows + 2, part, size), jnp.bfloat16),
                pltpu.VMEM((layers, len(needed[1]), rows + 2, part, size), jnp.bfloat16),
                pltpu.VMEM((diagonals, size, size), jnp.bfloat16),
                pltpu.VMEM((rows, layers, diagonals, part, size), jnp.bfloat16),
                pltpu.SemaphoreType.DMA,
                pltpu.SemaphoreType.DMA((rows,)),
                pltpu.SemaphoreType.DMA((rows,)),
                pltpu.SemaphoreType.DMA((rows,)),
                pltpu.SemaphoreType.DMA,
                pltpu.SemaphoreType.DMA,
            ],
            compiler_params=pltpu.CompilerParams(has_side_effects=True, vmem_limit_bytes=48 * 2**20),
        )(masked, presence)

    return jax.shard_map(
        per_device,
        mesh=mesh,
        in_specs=(P(None, ("row", "col"), "layer", None), P(None, ("row", "col"))),
        out_specs=P(None, ("row", "col"), "layer", None),
        check_vma=False,
    )
```
